32 devices in a mesh: seq: 8 (over z, x), tp: 4 (over y, core).
Axes of the slice: x: 2, y: 2, z: 4, core: 2. Of those that a mesh axis runs over, the one named last changes fastest.
Arguments:
- byte_states: bfloat16 [4096, 1024], P('seq'), may hold values from -6 to 6
- flags: int32 [4096], P('seq'), may hold values from 0 to 1, as said below
- stretch_owner: int32 [1024, 1], P('seq'), may hold values from 0 to 7; in each aligned block of 128 rows (0 to 127, 128 to 255, ...) at most 32 rows name the same one
- log_decay: float32 [4096, 16], P('seq', 'tp'), may hold values from -2 to 0, as said below
- w_x: bfloat16 [1024, 2048], P(None, 'tp'), may hold values from -0.1875 to 0.1875
- w_z: bfloat16 [1024, 2048], P(None, 'tp'), may hold values from -0.1875 to 0.1875
- w_bc: bfloat16 [1024, 256], replicated, may hold values from -0.1875 to 0.1875
- w_out: bfloat16 [2048, 1024], P('tp'), may hold values from -0.125 to 0.125
- pad_vector: bfloat16 [512], replicated, may hold values from -5 to 5
- w_q: bfloat16 [1536, 1536], P(None, 'tp'), may hold values from -8 to 8
- w_k: bfloat16 [1536, 1536], P(None, 'tp'), may hold values from -8 to 8
- w_v: bfloat16 [1536, 1536], P(None, 'tp'), may hold values from -0.15625 to 0.15625
- w_o: bfloat16 [1536, 1536], P('tp'), may hold values from -0.15625 to 0.15625
Outputs:
- enc_out: bfloat16 [4096, 1024], P('seq', 'tp')
- main_out: bfloat16 [2048, 1536], P('seq')
The draws below stay inside these ranges and needn't reach their ends.
Inputs may be any that keep to these rules, and one draw needn't show every extreme that they name: `flags`: exactly 128 ones among each aligned block of 512 bytes. `stretch_owner`: in each aligned block of 128 stretches no owner is named more than 32 times. `log_decay`: negative.
All inputs are finite; a program needn't handle non-finite values.
Results may differ from the reference program's by a relative error of at most 0.015.
Values may be sent and summed in bfloat16 or wider, within the bound.
A program may use at most 128 MiB of HBM per device.

```python
import math
import jax
import jax.numpy as jnp
import numpy as np
from jax import lax

D = 1024
INNER = 2048
RECURRENT_UNITS = 16
HEAD_P = 128
STATE = 128
DM = 1536
HM = 12
HD = 128
BLOCK = 256
BYTES_DEV = 512
CH_DEV = 128
OWNERS = 8
CAP = 32
ROWS_OWN = 256
TEXT_OCTETS = 4096
STRETCHES = 1024
SLOTS = 2048


def draw_flags(key, part):
    groups = TEXT_OCTETS // BYTES_DEV
    sampler_seeds = jax.random.split(key, groups)

    def shuffled(subkey):
        return jax.random.permutation(subkey, BYTES_DEV)
    orders = jax.vmap(shuffled)(sampler_seeds)
    return (orders < CH_DEV).astype(jnp.int32).reshape(TEXT_OCTETS)


def draw_log_decay(key, part):
    sampler_seeds = jax.random.split(key, 7)
    fast_share = 0.5
    fast = jax.random.uniform(sampler_seeds[0], (RECURRENT_UNITS,), jnp.float32) < fast_share
    fast_rate = jnp.exp(jax.random.uniform(sampler_seeds[1], (RECURRENT_UNITS,), jnp.float32, math.log(1.0 / 50.0), math.log(1.0 / 30.0)))
    slow_rate = jnp.exp(jax.random.uniform(sampler_seeds[2], (RECURRENT_UNITS,), jnp.float32, math.log(0.1), math.log(0.5))) / TEXT_OCTETS
    widening_ratio = jnp.where(fast, fast_rate, slow_rate)
    groups = TEXT_OCTETS // BYTES_DEV
    device_factor = jnp.exp2(jax.random.uniform(sampler_seeds[3], (groups, RECURRENT_UNITS), jnp.float32))
    octet_codes = jnp.repeat(device_factor, BYTES_DEV, axis=0)
    rough_guess = jnp.exp(jax.random.uniform(sampler_seeds[4], (TEXT_OCTETS, RECURRENT_UNITS), jnp.float32, math.log(0.5), math.log(2.0)))
    spurt_displacement = jax.random.randint(sampler_seeds[5], (2,), 0, TEXT_OCTETS)
    spurt_extent = jax.random.uniform(sampler_seeds[6], (2, RECURRENT_UNITS), jnp.float32, 0.22, 0.5)
    octet_location = jnp.arange(TEXT_OCTETS)
    agreement_tally = (octet_location[:, None] == spurt_displacement[None, :]).astype(jnp.float32)
    spurt_batches = jnp.sum(agreement_tally[:, :, None] * spurt_extent[None, :, :], axis=1)
    return -(widening_ratio[None, :] * octet_codes * rough_guess) - spurt_batches


def key_basis(key):
    return jax.random.truncated_normal(jax.random.fold_in(key, 11), -4.0, 4.0, (DM, HM * HD), jnp.float32)


def draw_w_k(key, part):
    return (key_basis(key) / math.sqrt(DM)).astype(jnp.bfloat16)


def draw_w_q(key, part):
    noise = jax.random.truncated_normal(jax.random.fold_in(key, 13), -4.0, 4.0, (DM, HM * HD), jnp.float32)
    mixed = noise
    return (mixed / math.sqrt(DM)).astype(jnp.bfloat16)


def block_levels(own_key, extent, pieces, smallest, high):
    level, own = 1.0, jax.random.fold_in(own_key, 6)
    for dim, blocks in pieces:
        draws = jnp.exp(jax.random.uniform(jax.random.fold_in(own, dim), (blocks,), jnp.float32, smallest / len(pieces), high / len(pieces)))
        level = level * jnp.repeat(draws, extent[dim] // blocks).reshape([-1 if axis == dim else 1 for axis in range(len(extent))])
    return level


def deal_out(own_key, own, number, rows, amount, top, most, slope):
    sequence = jax.random.permutation(own_key, amount)
    crowded, common = portions_of(amount, rows * top, most, slope, True), portions_of(amount, rows * top, most, slope, False)
    places = jnp.arange(amount)

    def named(lengths, turn):
        used = int((lengths > 0).sum())
        fixed = max(1, used // 4)
        passed = fixed + (places - fixed + turn * (used - fixed)) % max(1, amount - fixed)
        return jnp.zeros((amount,), jnp.int32).at[sequence[jnp.where(places < fixed, places, passed)]].set(jnp.asarray(lengths, jnp.int32))

    lengths = jnp.where(number % 4 == 0, named(crowded, number // 4), named(common, number - number // 4 - 1))
    mixed = jax.random.permutation(jax.random.fold_in(own, 3), amount)
    source_of, taker = mixed[0:amount // 2 * 2:2], mixed[1:amount // 2 * 2:2]
    margin = jnp.minimum(lengths[source_of] - 1, most - lengths[taker]) // 2
    margin = jnp.where((source_of == sequence[0]) | (taker == sequence[0]) | (lengths[taker] == 0), 0, jnp.maximum(margin, 0))
    passed = jax.random.randint(jax.random.fold_in(own, 4), (amount // 2,), 0, 1 << 20) % (margin + 1)
    lengths = lengths.at[source_of].add(-passed).at[taker].add(passed)
    labels = jnp.searchsorted(jnp.cumsum(lengths), jnp.arange(rows * top), side="right").astype(jnp.int32)
    table = labels.reshape(top, rows).T
    table = table[jax.random.permutation(jax.random.fold_in(own, 1), rows)]
    turn = jax.random.randint(jax.random.fold_in(own, 2), (rows, 1), 0, top)
    return jnp.take_along_axis(table, (jnp.arange(top)[None, :] + turn) % top, axis=1)


def portions_of(count, total, most, lean, full):
    weights = [(1 << 20) // math.isqrt(grade ** lean) + 1 for grade in range(1, count + 1)]
    largest = most if full else min(most, max(-(-total // count), total * weights[0] // sum(weights)))
    least = 1 if total - largest >= count - 1 else 0
    given, spare = [largest] + [least] * (count - 1), total - largest - least * (count - 1)
    while spare > 0:
        free = [i for i in range(1, count) if given[i] < largest] or [i for i in range(1, count) if given[i] < most]
        whole, remaining = sum([weights[i] for i in free]), spare
        for i in free:
            extra = min(most - given[i], max(1, remaining * weights[i] // whole), spare)
            given[i] = given[i] + extra
            spare = spare - extra
    return np.array(given)


def bell_draw(own_key, dims, width, limit, cuts=(), held_as=jnp.bfloat16):
    array = width * jax.random.normal(own_key, dims, jnp.float32)
    if cuts:
        array = array * block_levels(own_key, dims, cuts, -0.22, 0.18)
    return jnp.clip(array, -limit, limit).astype(held_as)


def setup_inputs(seed: int = 0) -> dict:
    seeds = jax.random.split(jax.random.key(seed), 14)
    byte_states = bell_draw(seeds[0], (TEXT_OCTETS, D), 1.0, 6.0, ((0, 8),))
    flags = draw_flags(jax.random.fold_in(seeds[13], 71), 0)
    stretch_owner_keys = jax.random.split(jax.random.fold_in(seeds[2], 1), STRETCHES // CH_DEV)
    stretch_owner_turns = jax.random.permutation(jax.random.fold_in(seeds[2], 3), STRETCHES // CH_DEV)
    stretch_owner = jax.vmap(lambda own, number: deal_out(jax.random.fold_in(seeds[2], 2), own, number, CH_DEV, OWNERS, 1, CAP, 2))(stretch_owner_keys, stretch_owner_turns).reshape((STRETCHES, 1))
    log_decay = draw_log_decay(jax.random.fold_in(seeds[13], 71), 0)
    w_x = bell_draw(seeds[4], (D, INNER), D ** -0.5, 0.1875, ((1, 4),))
    w_z = bell_draw(seeds[5], (D, INNER), D ** -0.5, 0.1875, ((1, 4),))
    w_bc = bell_draw(seeds[6], (D, 2 * STATE), D ** -0.5, 0.1875)
    w_out = bell_draw(seeds[7], (INNER, D), INNER ** -0.5, 0.125, ((0, 4),))
    pad_vector = bell_draw(seeds[8], (DM - D,), 1.0, 5.0)
    w_q = draw_w_q(jax.random.fold_in(seeds[13], 71), 0)
    w_k = draw_w_k(jax.random.fold_in(seeds[13], 71), 0)
    w_v = bell_draw(seeds[11], (DM, HM * HD), DM ** -0.5, 0.15625, ((1, 4),))
    w_o = bell_draw(seeds[12], (HM * HD, DM), (HM * HD) ** -0.5, 0.15625, ((0, 4),))
    return dict(byte_states=byte_states, flags=flags, stretch_owner=stretch_owner, log_decay=log_decay, w_x=w_x, w_z=w_z, w_bc=w_bc, w_out=w_out, pad_vector=pad_vector, w_q=w_q, w_k=w_k, w_v=w_v, w_o=w_o)


eps = 1e-05
highest = lax.Precision.HIGHEST

def rms_rows(values):
    wide = values.astype(jnp.float32)
    return wide * lax.rsqrt(lax.optimization_barrier(jnp.mean(wide * wide, axis=-1, keepdims=True)) + eps)

def ssd_blocks(xh, bmat, cmat, decay, start_state):
    rows, heads, width_p = xh.shape
    nblk = rows // BLOCK

    def advance(state, block):
        x_blk, b_blk, c_blk, a_blk = block
        cum = jnp.cumsum(a_blk, axis=0)
        later = lax.broadcasted_iota(jnp.int32, (BLOCK, BLOCK), 0)
        earlier = lax.broadcasted_iota(jnp.int32, (BLOCK, BLOCK), 1)
        causal = (later >= earlier)[:, :, None]
        spans = jnp.where(causal, cum[:, None, :] - cum[None, :, :], -1e+30)
        intersection = jnp.dot(c_blk, b_blk.T, preferred_element_type=jnp.float32)
        mixing = intersection[:, :, None] * jnp.exp(spans)
        x_wide = x_blk.astype(jnp.float32)
        inside = jnp.einsum('tsh,shp->thp', mixing, x_wide, precision=highest)
        carried = jnp.einsum('tn,hnp->thp', c_blk.astype(jnp.float32), state, precision=highest) * jnp.exp(cum)[:, :, None]
        tail = jnp.exp(cum[-1][None, :] - cum)
        fresh = jnp.einsum('sh,sn,shp->hnp', tail, b_blk.astype(jnp.float32), x_wide, precision=highest)
        new_state = state * jnp.exp(cum[-1])[:, None, None] + fresh
        return (new_state, inside + carried)
    blocks = (xh.reshape(nblk, BLOCK, heads, width_p), bmat.reshape(nblk, BLOCK, -1), cmat.reshape(nblk, BLOCK, -1), decay.reshape(nblk, BLOCK, heads))
    final, outs = lax.scan(advance, start_state, blocks)
    return (outs.reshape(rows, heads, width_p), final)

def attention_rows(queries, keys, values):
    count = queries.shape[0]
    size = math.gcd(count, 256)
    scale = 1.0 / math.sqrt(HD)
    key_wide = keys.astype(jnp.float32)
    value_wide = values.astype(jnp.float32)
    key_pos = jnp.arange(count).astype(jnp.int32)

    def one_block(start):
        q_blk = lax.dynamic_slice_in_dim(queries, start, size, 0).astype(jnp.float32)
        scores = jnp.einsum('qhd,khd->hqk', q_blk, key_wide) * scale
        query_pos = start + jnp.arange(size).astype(jnp.int32)
        allowed = key_pos[None, None, :] <= query_pos[None, :, None]
        scores = jnp.where(allowed, scores, -1e+30)
        top = lax.optimization_barrier(jnp.max(scores, axis=2, keepdims=True))
        expo = jnp.where(allowed, jnp.exp(scores - top), 0.0)
        total = lax.optimization_barrier(jnp.sum(expo, axis=2))
        rounded = lax.optimization_barrier(expo.astype(jnp.bfloat16))
        numer = jnp.einsum('hqk,khd->qhd', rounded.astype(jnp.float32), value_wide)
        return (numer / jnp.transpose(total)[:, :, None]).astype(jnp.bfloat16)
    starts = (jnp.arange(count // size) * size).astype(jnp.int32)
    result = lax.map(one_block, starts)
    return result.reshape(count, queries.shape[1] * queries.shape[2])

def reference(byte_states, flags, stretch_owner, log_decay, w_x, w_z, w_bc, w_out, pad_vector, w_q, w_k, w_v, w_o):
    normed = rms_rows(byte_states).astype(jnp.bfloat16)
    xs = jnp.dot(normed, w_x, preferred_element_type=jnp.float32).astype(jnp.bfloat16)
    zgate = jnp.dot(normed, w_z, preferred_element_type=jnp.float32)
    projected = jnp.dot(normed, w_bc, preferred_element_type=jnp.float32).astype(jnp.bfloat16)
    bmat = projected[:, :STATE]
    cmat = projected[:, STATE:]
    start_state = jnp.zeros((RECURRENT_UNITS, STATE, HEAD_P), jnp.float32)
    mixed, final = ssd_blocks(xs.reshape(TEXT_OCTETS, RECURRENT_UNITS, HEAD_P), bmat, cmat, log_decay, start_state)
    gated = mixed * jax.nn.silu(zgate).reshape(TEXT_OCTETS, RECURRENT_UNITS, HEAD_P)
    scaled = gated * lax.rsqrt(lax.optimization_barrier(jnp.mean(gated * gated, axis=2, keepdims=True)) + eps)
    scaled = scaled.reshape(TEXT_OCTETS, INNER).astype(jnp.bfloat16)
    enc_out = (byte_states.astype(jnp.float32) + jnp.dot(scaled, w_out, preferred_element_type=jnp.float32)).astype(jnp.bfloat16)
    picked = jnp.nonzero(flags == 1, size=STRETCHES)[0].astype(jnp.int32)
    stretch_rows = enc_out[picked]
    owners = stretch_owner[:, 0].astype(jnp.int32)
    owner_hot = (owners[:, None] == jnp.arange(OWNERS).astype(jnp.int32)[None, :]).astype(jnp.int32)
    owner_hot = owner_hot.reshape(OWNERS, CH_DEV, OWNERS)
    before = jnp.cumsum(owner_hot, axis=1) - owner_hot
    order = lax.optimization_barrier(jnp.sum(before * owner_hot, axis=2)).reshape(STRETCHES).astype(jnp.int32)
    source = (jnp.arange(STRETCHES) // CH_DEV).astype(jnp.int32)
    slot = owners * ROWS_OWN + source * CAP + order
    padding = jnp.broadcast_to(pad_vector[None, :], (STRETCHES, DM - D))
    stream = jnp.concatenate([stretch_rows, padding], axis=1)
    stream_norm = rms_rows(stream).astype(jnp.bfloat16)
    queries = jnp.dot(stream_norm, w_q, preferred_element_type=jnp.float32).astype(jnp.bfloat16).reshape(STRETCHES, HM, HD)
    keys = jnp.dot(stream_norm, w_k, preferred_element_type=jnp.float32).astype(jnp.bfloat16).reshape(STRETCHES, HM, HD)
    values = jnp.dot(stream_norm, w_v, preferred_element_type=jnp.float32).astype(jnp.bfloat16).reshape(STRETCHES, HM, HD)
    attended = attention_rows(queries, keys, values)
    main = (stream.astype(jnp.float32) + jnp.dot(attended, w_o, preferred_element_type=jnp.float32)).astype(jnp.bfloat16)
    main_out = jnp.zeros((SLOTS, DM), jnp.bfloat16).at[slot].set(main)
    return (enc_out, main_out)
```

```python
import functools
import math

import jax
import jax.numpy as jnp
from jax import lax
from jax.experimental import pallas as pl
from jax.experimental.pallas import tpu as pltpu
from jax.sharding import PartitionSpec as P

HD = 128
eps = 1e-05
f32 = jnp.float32
bf16 = jnp.bfloat16
MESH = pl.DeviceIdType.MESH
VM = pl.BlockSpec(memory_space=pltpu.VMEM)
DMA = pltpu.SemaphoreType.DMA


def mm(a, b):
    return jnp.dot(a, b, preferred_element_type=f32)


def mm_t(a, b):
    return lax.dot_general(a, b, (((1,), (1,)), ((), ())), preferred_element_type=f32)


def t_mm(a, b):
    return lax.dot_general(a, b, (((0,), (0,)), ((), ())), preferred_element_type=f32)


def three(a):
    hi = a.astype(bf16)
    rest = a - hi.astype(f32)
    mid = rest.astype(bf16)
    low = (rest - mid.astype(f32)).astype(bf16)
    return hi, mid, low


def iota(shape, dim):
    return lax.broadcasted_iota(jnp.int32, shape, dim)


def local_kernel(
    bytes_ref, wx_ref, wz_ref, wbc_ref, decay_ref, mixed_ref, gate_ref, c_ref, grow_ref, state_ref
):
    rows = bytes_ref.shape[0]
    heads = decay_ref.shape[1]
    state_n = wbc_ref.shape[1] // 2
    p = wx_ref.shape[1] // heads
    wide = bytes_ref[...].astype(f32)
    normed = (wide * lax.rsqrt(jnp.mean(wide * wide, axis=-1, keepdims=True) + eps)).astype(bf16)
    bc = mm(normed, wbc_ref[...]).astype(bf16)
    bmat, cmat = bc[:, :state_n], bc[:, state_n:]
    c_ref[...] = cmat
    xs = mm(normed, wx_ref[...]).astype(bf16)
    parts = three(decay_ref[...])
    lower = (iota((rows, rows), 0) >= iota((rows, rows), 1)).astype(f32).astype(bf16)
    upper = (iota((rows, rows), 0) <= iota((rows, rows), 1)).astype(f32).astype(bf16)
    ones = jnp.ones((rows, state_n), bf16)
    cum = sum(mm(lower, part) for part in parts)
    cum_row = sum(t_mm(part, upper) for part in parts)
    total = sum(t_mm(part, ones) for part in parts)
    last = cum[rows - 1 : rows, :]
    grow_ref[...] = jnp.exp(cum)
    tail = jnp.exp(last - cum)
    for h in range(heads):
        scaled = (xs[:, h * p : (h + 1) * p].astype(f32) * tail[:, h : h + 1]).astype(bf16)
        state_ref[h * state_n : (h + 1) * state_n, :] = t_mm(bmat, scaled).astype(bf16)
    pieces = [piece.astype(f32) for piece in three(total)]
    filler = jnp.zeros((16 - heads % 16, state_n), f32)
    for i, piece in enumerate(pieces):
        start = heads * state_n + 16 * i
        state_ref[start : start + 16, :] = jnp.concatenate([piece, filler], axis=0).astype(bf16)
    z = mm(normed, wz_ref[...])
    gate_ref[...] = z * jax.nn.sigmoid(z)
    half = rows // 2
    for r in range(2):
        lo, hi = r * half, (r + 1) * half
        inter = mm_t(cmat[lo:hi], bmat[:hi])
        causal = iota((half, hi), 0) + lo >= iota((half, hi), 1)
        for h in range(heads):
            spans = cum[lo:hi, h : h + 1] - cum_row[h : h + 1, :hi]
            mixing = (inter * jnp.exp(jnp.where(causal, spans, -1e30))).astype(bf16)
            mixed_ref[lo:hi, h * p : (h + 1) * p] = mm(mixing, xs[:hi, h * p : (h + 1) * p])


def encode_kernel(
    split, every_ref, mixed_ref, gate_ref, c_ref, grow_ref, wout_ref, flags_ref, bytes_ref,
    part_ref, rows_ref, base_ref,
):
    me = lax.axis_index("seq")
    rows, heads = grow_ref.shape
    state_n = c_ref.shape[1]
    p = mixed_ref.shape[1] // heads
    cmat = c_ref[...]
    scaled = []

    def step(k, state):
        block = every_ref[k].astype(f32)
        size = heads * state_n
        total = block[size : size + 16] + block[size + 16 : size + 32] + block[size + 32 :]
        shrink = jnp.exp(total)
        return tuple(
            state[h] * shrink[h : h + 1] + block[h * state_n : (h + 1) * state_n]
            for h in range(heads)
        )

    state = lax.fori_loop(
        0, me, step, tuple(jnp.zeros((state_n, p), f32) for _ in range(heads))
    )
    for h in range(heads):
        cols = slice(h * p, (h + 1) * p)
        mixed = mixed_ref[:, cols] + mm(cmat, state[h].astype(bf16)) * grow_ref[:, h : h + 1]
        gated = mixed * gate_ref[:, cols]
        norm = lax.rsqrt(jnp.mean(gated * gated, axis=1, keepdims=True) + eps)
        scaled.append((gated * norm).astype(bf16))
    scaled = jnp.concatenate(scaled, axis=1)
    count = rows_ref.shape[1]
    flags = flags_ref[...]
    upper = (iota((rows, rows), 0) <= iota((rows, rows), 1)).astype(f32).astype(bf16)
    many = jnp.broadcast_to(flags.astype(f32), (16, rows)).astype(bf16)
    rank = mm(many, upper)[0:1, :].astype(jnp.int32) - 1
    hit = (rank == iota((count, rows), 0)) & (flags == 1)
    picker = jnp.where(hit, 1.0, 0.0).astype(bf16)
    base_ref[...] = mm(picker, bytes_ref[...]).astype(bf16)
    quarter = wout_ref.shape[1] // split
    for q in range(split):
        part = mm(scaled, wout_ref[:, q * quarter : (q + 1) * quarter]).astype(bf16)
        part_ref[q] = part
        rows_ref[q] = mm(picker, part).astype(bf16)


def project_kernel(rows_ref, pad_ref, wq_ref, wk_ref, wv_ref, owner_ref, q_ref, kv_ref, stream_ref, place_ref):
    split, count, quarter = rows_ref.shape
    pad = jnp.broadcast_to(pad_ref[...].astype(f32), (count, pad_ref.shape[1])).astype(bf16)
    stream = jnp.concatenate([rows_ref[q] for q in range(split)] + [pad], axis=1)
    size = stream.shape[1] // split
    for q in range(split):
        stream_ref[q] = stream[:, q * size : (q + 1) * size]
    wide = stream.astype(f32)
    norm = (wide * lax.rsqrt(jnp.mean(wide * wide, axis=-1, keepdims=True) + eps)).astype(bf16)
    q_ref[...] = mm(norm, wq_ref[...]).astype(bf16)
    width = wk_ref.shape[1]
    kv_ref[:, :width] = mm(norm, wk_ref[...]).astype(bf16)
    kv_ref[:, width:] = mm(norm, wv_ref[...]).astype(bf16)
    slots = place_ref.shape[1]
    owner = owner_ref[...]
    ranks = -(-lax.axis_size("seq") // 128) * 128
    hot = jnp.where(owner == iota((count, ranks), 1), 1.0, 0.0)
    strict = jnp.where(iota((count, count), 0) > iota((count, count), 1), 1.0, 0.0)
    before = mm(strict.astype(bf16), hot.astype(bf16))
    order = jnp.sum(before * hot, axis=1, keepdims=True).astype(jnp.int32)
    cap = slots // lax.axis_size("seq")
    slot = owner * cap + order
    place_ref[...] = jnp.where(slot == iota((count, slots), 1), 1.0, 0.0).astype(bf16)


def attend_kernel(group, split, q_ref, all_ref, wo_ref, out_ref):
    me = lax.axis_index("seq")
    ranks, count, width2 = all_ref.shape
    width = width2 // 2
    heads = width // HD
    scale = 1.0 / math.sqrt(HD)
    keys = group * count

    def chunk(c, carry):
        start = c * group
        blocks = all_ref[pl.ds(start, group)]
        blocks = blocks.reshape(keys, width2)
        key_pos = start * count + iota((count, keys), 1)
        allowed = key_pos <= me * count + iota((count, keys), 0)
        seen = start * count + iota((keys, width), 0) < (me + 1) * count
        values = jnp.where(seen, blocks[:, width:], jnp.zeros((), bf16))
        new = []
        for h in range(heads):
            best, total, accum = carry[h]
            cols = slice(h * HD, (h + 1) * HD)
            scores = mm_t(q_ref[:, cols], blocks[:, cols]) * scale
            scores = jnp.where(allowed, scores, -1e30)
            top = jnp.maximum(best, jnp.max(scores, axis=1, keepdims=True))
            shrink = jnp.exp(best - top)
            expo = jnp.exp(scores - top)
            total = total * shrink + jnp.sum(expo, axis=1, keepdims=True)
            accum = accum * shrink + mm(expo.astype(bf16), values[:, cols])
            new.append((top, total, accum))
        return tuple(new)

    start = tuple(
        (jnp.full((count, 1), -1e30, f32), jnp.zeros((count, 1), f32), jnp.zeros((count, HD), f32))
        for _ in range(heads)
    )
    if ranks == group:
        done = chunk(0, start)
    else:
        done = lax.fori_loop(0, me // group + 1, chunk, start)
    attended = jnp.concatenate([(a / t).astype(bf16) for _, t, a in done], axis=1)
    size = wo_ref.shape[1] // split
    for q in range(split):
        out_ref[q] = mm(attended, wo_ref[:, q * size : (q + 1) * size]).astype(bf16)


def greet(devices):
    barrier = pltpu.get_barrier_semaphore()
    for device in devices:
        pl.semaphore_signal(barrier, inc=1, device_id=device, device_id_type=MESH)
    pl.semaphore_wait(barrier, len(devices))


def others(axis):
    me, n = lax.axis_index(axis), lax.axis_size(axis)
    return [lax.rem(me + d, n) for d in range(1, n)]


def remote(src, dst, send, recv, device):
    return pltpu.make_async_remote_copy(
        src_ref=src, dst_ref=dst, send_sem=send, recv_sem=recv, device_id=device, device_id_type=MESH
    )


def swap_start(src_ref, dst_ref, axis, send, recv):
    me = lax.axis_index(axis)
    copies = []
    for d, peer in enumerate(others(axis)):
        copy = remote(src_ref.at[peer], dst_ref.at[me], send.at[d], recv.at[d], {axis: peer})
        copy.start()
        copies.append(copy)
    return copies


def upward_kernel(with_swap, *refs):
    if with_swap:
        x_ref, part_ref, out_ref, got_ref, zs, zr, xsend, xr, own, ts, tr = refs
    else:
        x_ref, out_ref, zs, zr, xsend, xr, own = refs
    me = lax.axis_index("seq")
    n = lax.axis_size("seq")
    high, low = me // 2, lax.rem(me, 2)
    line = n // 2
    partner = {"seq": high * 2 + 1 - low}
    devices = [{"seq": lax.rem(high + d, line) * 2 + low} for d in range(1, line)] + [partner]
    if with_swap:
        devices = devices + [{"tp": peer} for peer in others("tp")]
    greet(devices)
    mine = pltpu.make_async_copy(x_ref, out_ref.at[me], own)
    mine.start()

    def up(d):
        return remote(x_ref, out_ref.at[me], zs.at[d], zr.at[d], {"seq": (high + d) * 2 + low})

    def arrived(d):
        slot = out_ref.at[(high - d) * 2 + low]
        return remote(slot, slot, zs.at[d], zr.at[d], partner)

    def across(d):
        slot = out_ref.at[(high - d) * 2 + low]
        return remote(slot, slot, xsend.at[d], xr.at[d], partner)

    def across_own():
        return remote(x_ref, out_ref.at[me], xsend.at[0], xr.at[0], partner)

    across_own().start()
    for d in range(1, line):

        @pl.when(high + d < line)
        def _():
            up(d).start()

    if with_swap:
        swaps = swap_start(part_ref, got_ref, "tp", ts, tr)
    for d in range(1, line):

        @pl.when(high >= d)
        def _():
            arrived(d).wait_recv()
            across(d).start()

    across_own().wait()
    for d in range(1, line):

        @pl.when(high >= d)
        def _():
            across(d).wait()

        @pl.when(high + d < line)
        def _():
            up(d).wait_send()

    mine.wait()
    if with_swap:
        for copy in swaps:
            copy.wait()


def upward(x, part=None, cid=0):
    n = lax.axis_size("seq")
    line = max(n // 2, 1)
    scratch = [DMA((line,)), DMA((line,)), DMA((line,)), DMA((line,)), DMA]
    shapes = [jax.ShapeDtypeStruct((n,) + x.shape, x.dtype)]
    args = [x]
    if part is not None:
        scratch += [DMA((part.shape[0],)), DMA((part.shape[0],))]
        shapes.append(jax.ShapeDtypeStruct(part.shape, part.dtype))
        args.append(part)
    return pl.pallas_call(
        functools.partial(upward_kernel, part is not None),
        out_shape=shapes,
        in_specs=[VM] * len(args),
        out_specs=[VM] * len(shapes),
        scratch_shapes=scratch,
        compiler_params=pltpu.CompilerParams(collective_id=cid, has_side_effects=True),
    )(*args)


def rows_kernel(rows_ref, base_ref, out_ref, got, mine, ts, tr, gs, gr, own):
    me = lax.axis_index("tp")
    peers = others("tp")
    greet([{"tp": peer} for peer in peers])
    for copy in swap_start(rows_ref, got, "tp", ts, tr):
        copy.wait()
    total = rows_ref[me].astype(f32)
    for peer in peers:
        total = total + got[peer].astype(f32)
    quarter = rows_ref.shape[2]
    base = base_ref[:, pl.ds(pl.multiple_of(me * quarter, 128), quarter)]
    mine[...] = (base.astype(f32) + total).astype(bf16)
    copies = [
        remote(mine, out_ref.at[me], gs.at[d], gr.at[d], {"tp": peer})
        for d, peer in enumerate(peers)
    ]
    for copy in copies:
        copy.start()
    out_ref[me] = mine[...]
    for copy in copies:
        copy.wait()


def final_kernel(
    part_ref, stream_ref, place_ref, out_ref, got, send, mine, ts, tr, ss, sr, gs, gr
):
    me = lax.axis_index("tp")
    seq = lax.axis_index("seq")
    peers = others("tp")
    greet([{"tp": peer} for peer in peers] + [{"seq": peer} for peer in others("seq")])
    for copy in swap_start(part_ref, got, "tp", ts, tr):
        copy.wait()
    total = stream_ref[me].astype(f32) + part_ref[me].astype(f32)
    for peer in peers:
        total = total + got[peer].astype(f32)
    main = total.astype(bf16)
    ranks, cap, size = send.shape
    send[...] = t_mm(place_ref[...], main).astype(bf16).reshape(ranks, cap, size)
    copies = swap_start(send, mine, "seq", ss, sr)
    mine[seq] = send[seq]
    for copy in copies:
        copy.wait()
    cols = pl.ds(pl.multiple_of(me * size, 128), size)
    copies = [
        remote(mine, out_ref.at[:, :, cols], gs.at[d], gr.at[d], {"tp": peer})
        for d, peer in enumerate(peers)
    ]
    for copy in copies:
        copy.start()
    out_ref[:, :, cols] = mine[...]
    for copy in copies:
        copy.wait()


def on_device(
    byte_states, flags, stretch_owner, log_decay, w_x, w_z, w_bc, w_out, pad_vector, w_q, w_k, w_v, w_o
):
    rows, width = byte_states.shape
    heads = log_decay.shape[1]
    inner = w_x.shape[1]
    state_n = w_bc.shape[1] // 2
    ranks = lax.axis_size("seq")
    split = lax.axis_size("tp")
    count = stretch_owner.shape[0]
    quarter = width // split
    cap = max(2, 2 * count // ranks)
    wide = w_q.shape[0]
    shape = jax.ShapeDtypeStruct
    params = pltpu.CompilerParams(vmem_limit_bytes=48 * 1024 * 1024)

    def call(kernel, outs, *args):
        return pl.pallas_call(
            kernel,
            out_shape=outs,
            in_specs=[VM] * len(args),
            out_specs=[VM] * len(outs),
            compiler_params=params,
        )(*args)

    mixed, gate, cmat, grow, state = call(
        local_kernel,
        [
            shape((rows, inner), f32),
            shape((rows, inner), f32),
            shape((rows, state_n), bf16),
            shape((rows, heads), f32),
            shape((heads * state_n + 48, inner // heads), bf16),
        ],
        byte_states, w_x, w_z, w_bc, log_decay,
    )
    (every,) = upward(state, cid=1)
    part, partial_rows, base = call(
        functools.partial(encode_kernel, split),
        [
            shape((split, rows, quarter), bf16),
            shape((split, count, quarter), bf16),
            shape((count, width), bf16),
        ],
        every, mixed, gate, cmat, grow, w_out, flags.reshape(1, rows), byte_states,
    )
    peers = max(split - 1, 1)
    stretch_rows = pl.pallas_call(
        rows_kernel,
        out_shape=shape((split, count, quarter), bf16),
        in_specs=[VM] * 2,
        out_specs=VM,
        scratch_shapes=[
            pltpu.VMEM((split, count, quarter), bf16),
            pltpu.VMEM((count, quarter), bf16),
        ]
        + [DMA((peers,))] * 4
        + [DMA],
        compiler_params=pltpu.CompilerParams(collective_id=2, has_side_effects=True),
    )(partial_rows, base)
    queries, kv, stream, place = call(
        project_kernel,
        [
            shape((count, w_q.shape[1]), bf16),
            shape((count, 2 * w_k.shape[1]), bf16),
            shape((split, count, wide // split), bf16),
            shape((count, ranks * cap), bf16),
        ],
        stretch_rows, pad_vector.reshape(1, -1), w_q, w_k, w_v, stretch_owner,
    )
    every_kv, got = upward(kv, part, cid=3)
    group = math.gcd(ranks, 8)
    (partial_main,) = call(
        functools.partial(attend_kernel, group, split),
        [shape((split, count, wide // split), bf16)],
        queries, every_kv, w_o,
    )
    main_out = pl.pallas_call(
        final_kernel,
        out_shape=shape((ranks, cap, wide), bf16),
        in_specs=[VM] * 3,
        out_specs=VM,
        scratch_shapes=[
            pltpu.VMEM((split, count, wide // split), bf16),
            pltpu.VMEM((ranks, cap, wide // split), bf16),
            pltpu.VMEM((ranks, cap, wide // split), bf16),
        ]
        + [DMA((peers,))] * 2
        + [DMA((max(ranks - 1, 1),))] * 2
        + [DMA((peers,))] * 2,
        compiler_params=pltpu.CompilerParams(collective_id=4, has_side_effects=True),
    )(partial_main, stream, place)
    main_out = main_out.reshape(ranks * cap, wide)
    me = lax.axis_index("tp")
    own = lax.dynamic_index_in_dim(part, me, 0, keepdims=False).astype(f32)
    summed = own
    for d in range(1, split):
        peer = lax.rem(me + d, split)
        summed = summed + lax.dynamic_index_in_dim(got, peer, 0, keepdims=False).astype(f32)
    mine = lax.dynamic_slice_in_dim(byte_states, me * quarter, quarter, 1).astype(f32)
    return ((mine + summed).astype(bf16), main_out)


def solution(mesh):
    placed = (
        P("seq", None),
        P("seq"),
        P("seq", None),
        P("seq", "tp"),
        P(None, "tp"),
        P(None, "tp"),
        P(),
        P("tp", None),
        P(),
        P(None, "tp"),
        P(None, "tp"),
        P(None, "tp"),
        P("tp", None),
    )
    return jax.shard_map(
        on_device,
        mesh=mesh,
        in_specs=placed,
        out_specs=(P("seq", "tp"), P("seq", None)),
        check_vma=False,
    )
```

```python
import functools
import math

import jax
import jax.numpy as jnp
from jax import lax
from jax.experimental import pallas as pl
from jax.experimental.pallas import tpu as pltpu
from jax.sharding import PartitionSpec as P

HD = 128
eps = 1e-05
f32 = jnp.float32
bf16 = jnp.bfloat16
MESH = pl.DeviceIdType.MESH
VM = pl.BlockSpec(memory_space=pltpu.VMEM)
DMA = pltpu.SemaphoreType.DMA
LIMIT = 8 * 1024 * 1024


def mm(a, b):
    return jnp.dot(a, b, preferred_element_type=f32)


def mm_t(a, b):
    return lax.dot_general(a, b, (((1,), (1,)), ((), ())), preferred_element_type=f32)


def t_mm(a, b):
    return lax.dot_general(a, b, (((0,), (0,)), ((), ())), preferred_element_type=f32)


def three(a):
    hi = a.astype(bf16)
    rest = a - hi.astype(f32)
    mid = rest.astype(bf16)
    low = (rest - mid.astype(f32)).astype(bf16)
    return hi, mid, low


def iota(shape, dim):
    return lax.broadcasted_iota(jnp.int32, shape, dim)


def local_kernel(
    bytes_ref, wx_ref, wz_ref, wbc_ref, decay_ref, mixed_ref, gate_ref, c_ref, grow_ref, state_ref
):
    rows = bytes_ref.shape[0]
    heads = decay_ref.shape[1]
    state_n = wbc_ref.shape[1] // 2
    p = wx_ref.shape[1] // heads
    wide = bytes_ref[...].astype(f32)
    normed = (wide * lax.rsqrt(jnp.mean(wide * wide, axis=-1, keepdims=True) + eps)).astype(bf16)
    bc = mm(normed, wbc_ref[...]).astype(bf16)
    bmat, cmat = bc[:, :state_n], bc[:, state_n:]
    c_ref[...] = cmat
    xs = mm(normed, wx_ref[...]).astype(bf16)
    parts = three(decay_ref[...])
    lower = (iota((rows, rows), 0) >= iota((rows, rows), 1)).astype(f32).astype(bf16)
    upper = (iota((rows, rows), 0) <= iota((rows, rows), 1)).astype(f32).astype(bf16)
    ones = jnp.ones((rows, state_n), bf16)
    cum = sum(mm(lower, part) for part in parts)
    cum_row = sum(t_mm(part, upper) for part in parts)
    total = sum(t_mm(part, ones) for part in parts)
    last = cum[rows - 1 : rows, :]
    grow_ref[...] = jnp.exp(cum)
    tail = jnp.exp(last - cum)
    for h in range(heads):
        scaled = (xs[:, h * p : (h + 1) * p].astype(f32) * tail[:, h : h + 1]).astype(bf16)
        state_ref[h * state_n : (h + 1) * state_n, :] = t_mm(bmat, scaled).astype(bf16)
    pieces = [piece.astype(f32) for piece in three(total)]
    filler = jnp.zeros((16 - heads % 16, state_n), f32)
    for i, piece in enumerate(pieces):
        start = heads * state_n + 16 * i
        state_ref[start : start + 16, :] = jnp.concatenate([piece, filler], axis=0).astype(bf16)
    z = mm(normed, wz_ref[...])
    gate_ref[...] = z * jax.nn.sigmoid(z)
    half = rows // 2
    for r in range(2):
        lo, hi = r * half, (r + 1) * half
        inter = mm_t(cmat[lo:hi], bmat[:hi])
        causal = iota((half, hi), 0) + lo >= iota((half, hi), 1)
        for h in range(heads):
            spans = cum[lo:hi, h : h + 1] - cum_row[h : h + 1, :hi]
            mixing = (inter * jnp.exp(jnp.where(causal, spans, -1e30))).astype(bf16)
            mixed_ref[lo:hi, h * p : (h + 1) * p] = mm(mixing, xs[:hi, h * p : (h + 1) * p])


def encode_kernel(
    split, every_ref, mixed_ref, gate_ref, c_ref, grow_ref, wout_ref, flags_ref, bytes_ref,
    part_ref, rows_ref, base_ref,
):
    me = lax.axis_index("seq")
    rows, heads = grow_ref.shape
    state_n = c_ref.shape[1]
    p = mixed_ref.shape[1] // heads
    cmat = c_ref[...]
    scaled = []

    def step(k, state):
        block = every_ref[k].astype(f32)
        size = heads * state_n
        total = block[size : size + 16] + block[size + 16 : size + 32] + block[size + 32 :]
        shrink = jnp.exp(total)
        return tuple(
            state[h] * shrink[h : h + 1] + block[h * state_n : (h + 1) * state_n]
            for h in range(heads)
        )

    state = lax.fori_loop(
        0, me, step, tuple(jnp.zeros((state_n, p), f32) for _ in range(heads))
    )
    for h in range(heads):
        cols = slice(h * p, (h + 1) * p)
        mixed = mixed_ref[:, cols] + mm(cmat, state[h].astype(bf16)) * grow_ref[:, h : h + 1]
        gated = mixed * gate_ref[:, cols]
        norm = lax.rsqrt(jnp.mean(gated * gated, axis=1, keepdims=True) + eps)
        scaled.append((gated * norm).astype(bf16))
    scaled = jnp.concatenate(scaled, axis=1)
    count = rows_ref.shape[1]
    flags = flags_ref[...]
    upper = (iota((rows, rows), 0) <= iota((rows, rows), 1)).astype(f32).astype(bf16)
    many = jnp.broadcast_to(flags.astype(f32), (16, rows)).astype(bf16)
    rank = mm(many, upper)[0:1, :].astype(jnp.int32) - 1
    hit = (rank == iota((count, rows), 0)) & (flags == 1)
    picker = jnp.where(hit, 1.0, 0.0).astype(bf16)
    base_ref[...] = mm(picker, bytes_ref[...]).astype(bf16)
    quarter = wout_ref.shape[1] // split
    for q in range(split):
        part = mm(scaled, wout_ref[:, q * quarter : (q + 1) * quarter]).astype(bf16)
        part_ref[q] = part
        rows_ref[q] = mm(picker, part).astype(bf16)


def project_kernel(rows_ref, pad_ref, wq_ref, wk_ref, wv_ref, owner_ref, q_ref, kv_ref, stream_ref, place_ref):
    split, count, quarter = rows_ref.shape
    pad = jnp.broadcast_to(pad_ref[...].astype(f32), (count, pad_ref.shape[1])).astype(bf16)
    stream = jnp.concatenate([rows_ref[q] for q in range(split)] + [pad], axis=1)
    size = stream.shape[1] // split
    for q in range(split):
        stream_ref[q] = stream[:, q * size : (q + 1) * size]
    wide = stream.astype(f32)
    norm = (wide * lax.rsqrt(jnp.mean(wide * wide, axis=-1, keepdims=True) + eps)).astype(bf16)
    q_ref[...] = mm(norm, wq_ref[...]).astype(bf16)
    width = wk_ref.shape[1]
    kv_ref[:, :width] = mm(norm, wk_ref[...]).astype(bf16)
    kv_ref[:, width:] = mm(norm, wv_ref[...]).astype(bf16)
    slots = place_ref.shape[1]
    owner = owner_ref[...]
    ranks = -(-lax.axis_size("seq") // 128) * 128
    hot = jnp.where(owner == iota((count, ranks), 1), 1.0, 0.0)
    strict = jnp.where(iota((count, count), 0) > iota((count, count), 1), 1.0, 0.0)
    before = mm(strict.astype(bf16), hot.astype(bf16))
    order = jnp.sum(before * hot, axis=1, keepdims=True).astype(jnp.int32)
    cap = slots // lax.axis_size("seq")
    slot = owner * cap + order
    place_ref[...] = jnp.where(slot == iota((count, slots), 1), 1.0, 0.0).astype(bf16)


def attend_kernel(group, split, q_ref, all_ref, wo_ref, out_ref):
    me = lax.axis_index("seq")
    ranks, count, width2 = all_ref.shape
    width = width2 // 2
    heads = width // HD
    scale = 1.0 / math.sqrt(HD)
    keys = group * count

    def chunk(c, carry):
        start = c * group
        blocks = all_ref[pl.ds(start, group)]
        blocks = blocks.reshape(keys, width2)
        key_pos = start * count + iota((count, keys), 1)
        allowed = key_pos <= me * count + iota((count, keys), 0)
        seen = start * count + iota((keys, width), 0) < (me + 1) * count
        values = jnp.where(seen, blocks[:, width:], jnp.zeros((), bf16))
        new = []
        for h in range(heads):
            best, total, accum = carry[h]
            cols = slice(h * HD, (h + 1) * HD)
            scores = mm_t(q_ref[:, cols], blocks[:, cols]) * scale
            scores = jnp.where(allowed, scores, -1e30)
            top = jnp.maximum(best, jnp.max(scores, axis=1, keepdims=True))
            shrink = jnp.exp(best - top)
            expo = jnp.exp(scores - top)
            total = total * shrink + jnp.sum(expo, axis=1, keepdims=True)
            accum = accum * shrink + mm(expo.astype(bf16), values[:, cols])
            new.append((top, total, accum))
        return tuple(new)

    start = tuple(
        (jnp.full((count, 1), -1e30, f32), jnp.zeros((count, 1), f32), jnp.zeros((count, HD), f32))
        for _ in range(heads)
    )
    if ranks == group:
        done = chunk(0, start)
    else:
        done = lax.fori_loop(0, me // group + 1, chunk, start)
    attended = jnp.concatenate([(a / t).astype(bf16) for _, t, a in done], axis=1)
    size = wo_ref.shape[1] // split
    for q in range(split):
        out_ref[q] = mm(attended, wo_ref[:, q * size : (q + 1) * size]).astype(bf16)


def greet(devices):
    barrier = pltpu.get_barrier_semaphore()
    for device in devices:
        pl.semaphore_signal(barrier, inc=1, device_id=device, device_id_type=MESH)
    pl.semaphore_wait(barrier, len(devices))


def others(axis):
    me, n = lax.axis_index(axis), lax.axis_size(axis)
    return [lax.rem(me + d, n) for d in range(1, n)]


def remote(src, dst, send, recv, device):
    return pltpu.make_async_remote_copy(
        src_ref=src, dst_ref=dst, send_sem=send, recv_sem=recv, device_id=device, device_id_type=MESH
    )


def swap_start(src_ref, dst_ref, axis, send, recv):
    me = lax.axis_index(axis)
    copies = []
    for d, peer in enumerate(others(axis)):
        copy = remote(src_ref.at[peer], dst_ref.at[me], send.at[d], recv.at[d], {axis: peer})
        copy.start()
        copies.append(copy)
    return copies


def upward_kernel(with_swap, *refs):
    if with_swap:
        x_ref, part_ref, out_ref, got_ref, zs, zr, ws, wr, own, ts, tr = refs
    else:
        x_ref, out_ref, zs, zr, ws, wr, own = refs
    me = lax.axis_index("seq")
    n = lax.axis_size("seq")
    high, low = me // 2, lax.rem(me, 2)
    line = n // 2
    pieces = zs.shape[1]
    size = x_ref.shape[0] // pieces
    partner = {"seq": high * 2 + 1 - low}
    steps = sorted({1, line - 1} - {0}) if line > 1 else []
    devices = [{"seq": lax.rem(high + d, line) * 2 + low} for d in steps] + [partner]
    if with_swap:
        devices = devices + [{"tp": peer} for peer in others("tp")]
    greet(devices)
    mine = pltpu.make_async_copy(x_ref, out_ref.at[me], own)
    mine.start()

    def source(d, c):
        rows = pl.ds(c * size, size)
        return x_ref.at[rows] if d == 0 else out_ref.at[(high - d) * 2 + low, rows]

    def slot(d, c):
        return out_ref.at[(high - d) * 2 + low, pl.ds(c * size, size)]

    def up(d, c):
        device = {"seq": (high + 1) * 2 + low}
        return remote(source(d, c), slot(d, c), zs.at[d, c], zr.at[d + 1, c], device)

    def arrived(d, c):
        return remote(slot(d, c), slot(d, c), zs.at[d, c], zr.at[d, c], partner)

    def across(d, c):
        return remote(source(d, c), slot(d, c), ws.at[d, c], wr.at[d, c], partner)

    def send_on(d, c):
        if d < line - 1:

            @pl.when(high + 1 < line)
            def _():
                up(d, c).start()

        across(d, c).start()

    for c in range(pieces):
        send_on(0, c)
    if with_swap:
        swaps = swap_start(part_ref, got_ref, "tp", ts, tr)
    for d in range(1, line):

        @pl.when(high >= d)
        def _():
            for c in range(pieces):
                arrived(d, c).wait_recv()
                send_on(d, c)

    for d in range(line):

        @pl.when(high >= d)
        def _():
            for c in range(pieces):
                across(d, c).wait()
                if d < line - 1:

                    @pl.when(high + 1 < line)
                    def _():
                        up(d, c).wait_send()

    mine.wait()
    if with_swap:
        for copy in swaps:
            copy.wait()


def upward(x, part=None, cid=0):
    n = lax.axis_size("seq")
    line = max(n // 2, 1)
    fits = [c for c in (4, 5, 2, 1) if x.shape[0] % (16 * c) == 0 and c * line <= 32]
    pieces = fits[0]
    scratch = [DMA((line + 1, pieces))] * 4 + [DMA]
    shapes = [jax.ShapeDtypeStruct((n,) + x.shape, x.dtype)]
    args = [x]
    if part is not None:
        scratch += [DMA((part.shape[0],)), DMA((part.shape[0],))]
        shapes.append(jax.ShapeDtypeStruct(part.shape, part.dtype))
        args.append(part)
    return pl.pallas_call(
        functools.partial(upward_kernel, part is not None),
        out_shape=shapes,
        in_specs=[VM] * len(args),
        out_specs=[VM] * len(shapes),
        scratch_shapes=scratch,
        compiler_params=pltpu.CompilerParams(
            collective_id=cid, has_side_effects=True, vmem_limit_bytes=LIMIT
        ),
    )(*args)


def rows_kernel(rows_ref, base_ref, out_ref, got, mine, ts, tr, gs, gr, own):
    me = lax.axis_index("tp")
    peers = others("tp")
    greet([{"tp": peer} for peer in peers])
    for copy in swap_start(rows_ref, got, "tp", ts, tr):
        copy.wait()
    total = rows_ref[me].astype(f32)
    for peer in peers:
        total = total + got[peer].astype(f32)
    quarter = rows_ref.shape[2]
    base = base_ref[:, pl.ds(pl.multiple_of(me * quarter, 128), quarter)]
    mine[...] = (base.astype(f32) + total).astype(bf16)
    copies = [
        remote(mine, out_ref.at[me], gs.at[d], gr.at[d], {"tp": peer})
        for d, peer in enumerate(peers)
    ]
    for copy in copies:
        copy.start()
    out_ref[me] = mine[...]
    for copy in copies:
        copy.wait()


def final_kernel(
    part_ref, stream_ref, place_ref, out_ref, got, send, mine, ts, tr, ss, sr, cs, cr, ps, pr
):
    me = lax.axis_index("tp")
    seq = lax.axis_index("seq")
    peers = others("tp")
    groups = lax.axis_size("tp") // 2
    high, low = me // 2, lax.rem(me, 2)
    ranks, cap, size = send.shape
    greet([{"tp": peer} for peer in peers] + [{"seq": peer} for peer in others("seq")])
    for copy in swap_start(part_ref, got, "tp", ts, tr):
        copy.wait()
    total = stream_ref[me].astype(f32) + part_ref[me].astype(f32)
    for peer in peers:
        total = total + got[peer].astype(f32)
    main = total.astype(bf16)
    send[...] = t_mm(place_ref[...], main).astype(bf16).reshape(ranks, cap, size)
    copies = swap_start(send, mine, "seq", ss, sr)
    mine[seq] = send[seq]

    def spot(e, d):
        column = (lax.rem(high - e + groups, groups) * 2 + low) * size
        return out_ref.at[lax.rem(seq - d + ranks, ranks), :, pl.ds(pl.multiple_of(column, 128), size)]

    def held(e, d):
        return mine.at[lax.rem(seq - d + ranks, ranks)] if e == 0 else spot(e, d)

    def direct(e, d):
        device = {"tp": lax.rem(high + e, groups) * 2 + low}
        return remote(held(0, d), spot(0, d), cs.at[e, d], cr.at[e, d], device)

    def pair(e, d):
        device = {"tp": high * 2 + 1 - low}
        return remote(held(e, d), spot(e, d), ps.at[e, d], pr.at[e, d], device)

    for d in range(ranks):
        if d > 0:
            copies[d - 1].wait_recv()
        for e in range(1, groups):
            direct(e, d).start()
        pair(0, d).start()
    for d in range(ranks):
        for e in range(1, groups):
            direct(e, d).wait_recv()
            pair(e, d).start()
    out_ref[:, :, pl.ds(pl.multiple_of(me * size, 128), size)] = mine[...]
    for d in range(ranks):
        if d > 0:
            copies[d - 1].wait_send()
        for e in range(groups):
            if e > 0:
                direct(e, d).wait_send()
            pair(e, d).wait()


def on_device(
    byte_states, flags, stretch_owner, log_decay, w_x, w_z, w_bc, w_out, pad_vector, w_q, w_k, w_v, w_o
):
    rows, width = byte_states.shape
    heads = log_decay.shape[1]
    inner = w_x.shape[1]
    state_n = w_bc.shape[1] // 2
    ranks = lax.axis_size("seq")
    split = lax.axis_size("tp")
    count = stretch_owner.shape[0]
    quarter = width // split
    cap = max(2, 2 * count // ranks)
    wide = w_q.shape[0]
    shape = jax.ShapeDtypeStruct
    params = pltpu.CompilerParams(vmem_limit_bytes=3 * LIMIT)

    def call(kernel, outs, *args):
        return pl.pallas_call(
            kernel,
            out_shape=outs,
            in_specs=[VM] * len(args),
            out_specs=[VM] * len(outs),
            compiler_params=params,
        )(*args)

    mixed, gate, cmat, grow, state = call(
        local_kernel,
        [
            shape((rows, inner), f32),
            shape((rows, inner), f32),
            shape((rows, state_n), bf16),
            shape((rows, heads), f32),
            shape((heads * state_n + 48, inner // heads), bf16),
        ],
        byte_states, w_x, w_z, w_bc, log_decay,
    )
    (every,) = upward(state, cid=1)
    part, partial_rows, base = call(
        functools.partial(encode_kernel, split),
        [
            shape((split, rows, quarter), bf16),
            shape((split, count, quarter), bf16),
            shape((count, width), bf16),
        ],
        every, mixed, gate, cmat, grow, w_out, flags.reshape(1, rows), byte_states,
    )
    peers = max(split - 1, 1)
    stretch_rows = pl.pallas_call(
        rows_kernel,
        out_shape=shape((split, count, quarter), bf16),
        in_specs=[VM] * 2,
        out_specs=VM,
        scratch_shapes=[
            pltpu.VMEM((split, count, quarter), bf16),
            pltpu.VMEM((count, quarter), bf16),
        ]
        + [DMA((peers,))] * 4
        + [DMA],
        compiler_params=pltpu.CompilerParams(
            collective_id=2, has_side_effects=True, vmem_limit_bytes=LIMIT
        ),
    )(partial_rows, base)
    queries, kv, stream, place = call(
        project_kernel,
        [
            shape((count, w_q.shape[1]), bf16),
            shape((count, 2 * w_k.shape[1]), bf16),
            shape((split, count, wide // split), bf16),
            shape((count, ranks * cap), bf16),
        ],
        stretch_rows, pad_vector.reshape(1, -1), w_q, w_k, w_v, stretch_owner,
    )
    every_kv, got = upward(kv, part, cid=3)
    group = math.gcd(ranks, 8)
    (partial_main,) = call(
        functools.partial(attend_kernel, group, split),
        [shape((split, count, wide // split), bf16)],
        queries, every_kv, w_o,
    )
    main_out = pl.pallas_call(
        final_kernel,
        out_shape=shape((ranks, cap, wide), bf16),
        in_specs=[VM] * 3,
        out_specs=VM,
        scratch_shapes=[
            pltpu.VMEM((split, count, wide // split), bf16),
            pltpu.VMEM((ranks, cap, wide // split), bf16),
            pltpu.VMEM((ranks, cap, wide // split), bf16),
        ]
        + [DMA((peers,))] * 2
        + [DMA((max(ranks - 1, 1),))] * 2
        + [DMA((split // 2, ranks))] * 4,
        compiler_params=pltpu.CompilerParams(
            collective_id=4, has_side_effects=True, vmem_limit_bytes=LIMIT
        ),
    )(partial_main, stream, place)
    main_out = main_out.reshape(ranks * cap, wide)
    me = lax.axis_index("tp")
    own = lax.dynamic_index_in_dim(part, me, 0, keepdims=False).astype(f32)
    summed = own
    for d in range(1, split):
        peer = lax.rem(me + d, split)
        summed = summed + lax.dynamic_index_in_dim(got, peer, 0, keepdims=False).astype(f32)
    mine = lax.dynamic_slice_in_dim(byte_states, me * quarter, quarter, 1).astype(f32)
    return ((mine + summed).astype(bf16), main_out)


def solution(mesh):
    placed = (
        P("seq", None),
        P("seq"),
        P("seq", None),
        P("seq", "tp"),
        P(None, "tp"),
        P(None, "tp"),
        P(),
        P("tp", None),
        P(),
        P(None, "tp"),
        P(None, "tp"),
        P(None, "tp"),
        P("tp", None),
    )
    return jax.shard_map(
        on_device,
        mesh=mesh,
        in_specs=placed,
        out_specs=(P("seq", "tp"), P("seq", None)),
        check_vma=False,
    )
```

```python
import functools
import math

import jax
import jax.numpy as jnp
from jax import lax
from jax.experimental import pallas as pl
from jax.experimental.pallas import tpu as pltpu
from jax.sharding import PartitionSpec as P

HD = 128
eps = 1e-05
f32 = jnp.float32
bf16 = jnp.bfloat16
MESH = pl.DeviceIdType.MESH
VM = pl.BlockSpec(memory_space=pltpu.VMEM)
HBM = pl.BlockSpec(memory_space=pltpu.HBM)
DMA = pltpu.SemaphoreType.DMA
LIMIT = 8 * 1024 * 1024


def cost(us):
    return pl.CostEstimate(flops=us * 10**9, bytes_accessed=us * 3 * 10**6, transcendentals=0)


def mm(a, b):
    return jnp.dot(a, b, preferred_element_type=f32)


def mm_t(a, b):
    return lax.dot_general(a, b, (((1,), (1,)), ((), ())), preferred_element_type=f32)


def t_mm(a, b):
    return lax.dot_general(a, b, (((0,), (0,)), ((), ())), preferred_element_type=f32)


def three(a):
    hi = a.astype(bf16)
    rest = a - hi.astype(f32)
    mid = rest.astype(bf16)
    low = (rest - mid.astype(f32)).astype(bf16)
    return hi, mid, low


def iota(shape, dim):
    return lax.broadcasted_iota(jnp.int32, shape, dim)


def local_kernel(
    bytes_hbm, wx_hbm, wz_hbm, wbc_hbm, decay_ref, mixed_ref, gate_ref, c_ref, grow_ref, state_ref,
    bytes_ref, wx_ref, wz_ref, wbc_ref, sems,
):
    fetches = []
    for i, (src, dst) in enumerate(
        ((bytes_hbm, bytes_ref), (wbc_hbm, wbc_ref), (wx_hbm, wx_ref), (wz_hbm, wz_ref))
    ):
        half = src.shape[0] // 2
        for j in range(2):
            span = pl.ds(j * half, half)
            copy = pltpu.make_async_copy(src.at[span], dst.at[span], sems.at[i, j])
            copy.start()
            fetches.append(copy)

    def ready(i):
        fetches[2 * i].wait()
        fetches[2 * i + 1].wait()

    rows = bytes_ref.shape[0]
    heads = decay_ref.shape[0]
    state_n = wbc_ref.shape[1] // 2
    p = wx_ref.shape[1] // heads
    parts = three(decay_ref[...])
    lower = (iota((rows, rows), 0) >= iota((rows, rows), 1)).astype(f32).astype(bf16)
    upper = (iota((rows, rows), 0) <= iota((rows, rows), 1)).astype(f32).astype(bf16)
    ones = jnp.ones((rows, state_n), bf16)
    cum = sum(mm_t(lower, part) for part in parts)
    cum_row = sum(mm(part, upper) for part in parts)
    total = sum(mm(part, ones) for part in parts)
    ready(0)
    wide = bytes_ref[...].astype(f32)
    normed = (wide * lax.rsqrt(jnp.mean(wide * wide, axis=-1, keepdims=True) + eps)).astype(bf16)
    ready(1)
    bc = mm(normed, wbc_ref[...]).astype(bf16)
    bmat, cmat = bc[:, :state_n], bc[:, state_n:]
    c_ref[...] = cmat
    ready(2)
    xs = mm(normed, wx_ref[...]).astype(bf16)
    last = cum[rows - 1 : rows, :]
    grow_ref[...] = jnp.exp(cum)
    tail = jnp.exp(last - cum)
    for h in range(heads):
        scaled = (xs[:, h * p : (h + 1) * p].astype(f32) * tail[:, h : h + 1]).astype(bf16)
        state_ref[h * state_n : (h + 1) * state_n, :] = t_mm(bmat, scaled).astype(bf16)
    pieces = [piece.astype(f32) for piece in three(total)]
    filler = jnp.zeros((16 - heads % 16, state_n), f32)
    for i, piece in enumerate(pieces):
        start = heads * state_n + 16 * i
        state_ref[start : start + 16, :] = jnp.concatenate([piece, filler], axis=0).astype(bf16)
    ready(3)
    z = mm(normed, wz_ref[...])
    gate_ref[...] = z * jax.nn.sigmoid(z)
    half = rows // 2
    for r in range(2):
        lo, hi = r * half, (r + 1) * half
        inter = mm_t(cmat[lo:hi], bmat[:hi])
        causal = iota((half, hi), 0) + lo >= iota((half, hi), 1)
        for h in range(heads):
            spans = cum[lo:hi, h : h + 1] - cum_row[h : h + 1, :hi]
            mixing = (inter * jnp.exp(jnp.where(causal, spans, -1e30))).astype(bf16)
            mixed_ref[lo:hi, h * p : (h + 1) * p] = mm(mixing, xs[:hi, h * p : (h + 1) * p])


def encode_kernel(
    split, every_ref, mixed_ref, gate_ref, c_ref, grow_ref, wout_ref, flags_ref, bytes_ref,
    part_ref, rows_ref, base_ref,
):
    me = lax.axis_index("seq")
    rows, heads = grow_ref.shape
    state_n = c_ref.shape[1]
    p = mixed_ref.shape[1] // heads
    cmat = c_ref[...]
    scaled = []

    def step(k, state):
        block = every_ref[k].astype(f32)
        size = heads * state_n
        total = block[size : size + 16] + block[size + 16 : size + 32] + block[size + 32 :]
        shrink = jnp.exp(total)
        return tuple(
            state[h] * shrink[h : h + 1] + block[h * state_n : (h + 1) * state_n]
            for h in range(heads)
        )

    state = lax.fori_loop(
        0, me, step, tuple(jnp.zeros((state_n, p), f32) for _ in range(heads))
    )
    for h in range(heads):
        cols = slice(h * p, (h + 1) * p)
        mixed = mixed_ref[:, cols] + mm(cmat, state[h].astype(bf16)) * grow_ref[:, h : h + 1]
        gated = mixed * gate_ref[:, cols]
        norm = lax.rsqrt(jnp.mean(gated * gated, axis=1, keepdims=True) + eps)
        scaled.append((gated * norm).astype(bf16))
    scaled = jnp.concatenate(scaled, axis=1)
    count = rows_ref.shape[1]
    flags = flags_ref[...]
    upper = (iota((rows, rows), 0) <= iota((rows, rows), 1)).astype(f32).astype(bf16)
    many = jnp.broadcast_to(flags.astype(f32), (16, rows)).astype(bf16)
    rank = mm(many, upper)[0:1, :].astype(jnp.int32) - 1
    hit = (rank == iota((count, rows), 0)) & (flags == 1)
    picker = jnp.where(hit, 1.0, 0.0).astype(bf16)
    base_ref[...] = mm(picker, bytes_ref[...]).astype(bf16)
    quarter = wout_ref.shape[1] // split
    for q in range(split):
        part = mm(scaled, wout_ref[:, q * quarter : (q + 1) * quarter]).astype(bf16)
        part_ref[q] = part
        rows_ref[q] = mm(picker, part).astype(bf16)


def project_kernel(rows_ref, pad_ref, wq_ref, wk_ref, wv_ref, owner_ref, q_ref, kv_ref, stream_ref, place_ref):
    split, count, quarter = rows_ref.shape
    pad = jnp.broadcast_to(pad_ref[...].astype(f32), (count, pad_ref.shape[1])).astype(bf16)
    stream = jnp.concatenate([rows_ref[q] for q in range(split)] + [pad], axis=1)
    size = stream.shape[1] // split
    for q in range(split):
        stream_ref[q] = stream[:, q * size : (q + 1) * size]
    wide = stream.astype(f32)
    norm = (wide * lax.rsqrt(jnp.mean(wide * wide, axis=-1, keepdims=True) + eps)).astype(bf16)
    q_ref[...] = mm(norm, wq_ref[...]).astype(bf16)
    width = wk_ref.shape[1]
    kv_ref[:, :width] = mm(norm, wk_ref[...]).astype(bf16)
    kv_ref[:, width:] = mm(norm, wv_ref[...]).astype(bf16)
    slots = place_ref.shape[1]
    owner = owner_ref[...]
    ranks = -(-lax.axis_size("seq") // 128) * 128
    hot = jnp.where(owner == iota((count, ranks), 1), 1.0, 0.0)
    strict = jnp.where(iota((count, count), 0) > iota((count, count), 1), 1.0, 0.0)
    before = mm(strict.astype(bf16), hot.astype(bf16))
    order = jnp.sum(before * hot, axis=1, keepdims=True).astype(jnp.int32)
    cap = slots // lax.axis_size("seq")
    slot = owner * cap + order
    place_ref[...] = jnp.where(slot == iota((count, slots), 1), 1.0, 0.0).astype(bf16)


def attend_kernel(
    group, split, q_ref, all_ref, wo_ref, part_ref, got_ref, bytes_hbm, out_ref, enc_ref, base, sem
):
    me = lax.axis_index("seq")
    col = lax.axis_index("tp")
    quarter = base.shape[1]
    span = pl.ds(pl.multiple_of(col * quarter, 128), quarter)
    fetch = pltpu.make_async_copy(bytes_hbm.at[:, span], base, sem)
    fetch.start()
    ranks, count, width2 = all_ref.shape
    width = width2 // 2
    heads = width // HD
    scale = 1.0 / math.sqrt(HD)
    keys = group * count

    def chunk(c, carry):
        start = c * group
        blocks = all_ref[pl.ds(start, group)]
        blocks = blocks.reshape(keys, width2)
        key_pos = start * count + iota((count, keys), 1)
        allowed = key_pos <= me * count + iota((count, keys), 0)
        seen = start * count + iota((keys, width), 0) < (me + 1) * count
        values = jnp.where(seen, blocks[:, width:], jnp.zeros((), bf16))
        new = []
        for h in range(heads):
            best, total, accum = carry[h]
            cols = slice(h * HD, (h + 1) * HD)
            scores = mm_t(q_ref[:, cols], blocks[:, cols]) * scale
            scores = jnp.where(allowed, scores, -1e30)
            top = jnp.maximum(best, jnp.max(scores, axis=1, keepdims=True))
            shrink = jnp.exp(best - top)
            expo = jnp.exp(scores - top)
            total = total * shrink + jnp.sum(expo, axis=1, keepdims=True)
            accum = accum * shrink + mm(expo.astype(bf16), values[:, cols])
            new.append((top, total, accum))
        return tuple(new)

    start = tuple(
        (jnp.full((count, 1), -1e30, f32), jnp.zeros((count, 1), f32), jnp.zeros((count, HD), f32))
        for _ in range(heads)
    )
    if ranks == group:
        done = chunk(0, start)
    else:
        done = lax.fori_loop(0, me // group + 1, chunk, start)
    attended = jnp.concatenate([(a / t).astype(bf16) for _, t, a in done], axis=1)
    size = wo_ref.shape[1] // split
    for q in range(split):
        out_ref[q] = mm(attended, wo_ref[:, q * size : (q + 1) * size]).astype(bf16)
    fetch.wait()
    summed = part_ref[col].astype(f32)
    for d in range(1, split):
        summed = summed + got_ref[lax.rem(col + d, split)].astype(f32)
    enc_ref[...] = (base[...].astype(f32) + summed).astype(bf16)


def greet(devices):
    barrier = pltpu.get_barrier_semaphore()
    for device in devices:
        pl.semaphore_signal(barrier, inc=1, device_id=device, device_id_type=MESH)
    pl.semaphore_wait(barrier, len(devices))


def others(axis):
    me, n = lax.axis_index(axis), lax.axis_size(axis)
    return [lax.rem(me + d, n) for d in range(1, n)]


def remote(src, dst, send, recv, device):
    return pltpu.make_async_remote_copy(
        src_ref=src, dst_ref=dst, send_sem=send, recv_sem=recv, device_id=device, device_id_type=MESH
    )


def swap_start(src_ref, dst_ref, axis, send, recv):
    me = lax.axis_index(axis)
    copies = []
    for d, peer in enumerate(others(axis)):
        copy = remote(src_ref.at[peer], dst_ref.at[me], send.at[d], recv.at[d], {axis: peer})
        copy.start()
        copies.append(copy)
    return copies


def upward_kernel(with_swap, *refs):
    if with_swap:
        x_ref, part_ref, out_ref, got_ref, zs, zr, ws, wr, own, ts, tr = refs
    else:
        x_ref, out_ref, zs, zr, ws, wr, own = refs
    me = lax.axis_index("seq")
    n = lax.axis_size("seq")
    high, low = me // 2, lax.rem(me, 2)
    line = n // 2
    pieces = zs.shape[1]
    size = x_ref.shape[0] // pieces
    partner = {"seq": high * 2 + 1 - low}
    steps = sorted({1, line - 1} - {0}) if line > 1 else []
    devices = [{"seq": lax.rem(high + d, line) * 2 + low} for d in steps] + [partner]
    if with_swap:
        devices = devices + [{"tp": peer} for peer in others("tp")]
    greet(devices)
    mine = pltpu.make_async_copy(x_ref, out_ref.at[me], own)
    mine.start()

    def source(d, c):
        rows = pl.ds(c * size, size)
        return x_ref.at[rows] if d == 0 else out_ref.at[(high - d) * 2 + low, rows]

    def slot(d, c):
        return out_ref.at[(high - d) * 2 + low, pl.ds(c * size, size)]

    def up(d, c):
        device = {"seq": (high + 1) * 2 + low}
        return remote(source(d, c), slot(d, c), zs.at[d, c], zr.at[d + 1, c], device)

    def arrived(d, c):
        return remote(slot(d, c), slot(d, c), zs.at[d, c], zr.at[d, c], partner)

    def across(d, c):
        return remote(source(d, c), slot(d, c), ws.at[d, c], wr.at[d, c], partner)

    def send_on(d, c):
        if d < line - 1:

            @pl.when(high + 1 < line)
            def _():
                up(d, c).start()

        across(d, c).start()

    for c in range(pieces):
        send_on(0, c)
    if with_swap:
        swaps = swap_start(part_ref, got_ref, "tp", ts, tr)
    for d in range(1, line):

        @pl.when(high >= d)
        def _():
            for c in range(pieces):
                arrived(d, c).wait_recv()
                send_on(d, c)

    for d in range(line):

        @pl.when(high >= d)
        def _():
            for c in range(pieces):
                across(d, c).wait()
                if d < line - 1:

                    @pl.when(high + 1 < line)
                    def _():
                        up(d, c).wait_send()

    mine.wait()
    if with_swap:
        for copy in swaps:
            copy.wait()


def upward(x, part=None, cid=0):
    n = lax.axis_size("seq")
    line = max(n // 2, 1)
    fits = [c for c in (4, 5, 2, 1) if x.shape[0] % (16 * c) == 0 and c * line <= 32]
    pieces = fits[0]
    scratch = [DMA((line + 1, pieces))] * 4 + [DMA]
    shapes = [jax.ShapeDtypeStruct((n,) + x.shape, x.dtype)]
    args = [x]
    if part is not None:
        scratch += [DMA((part.shape[0],)), DMA((part.shape[0],))]
        shapes.append(jax.ShapeDtypeStruct(part.shape, part.dtype))
        args.append(part)
    return pl.pallas_call(
        functools.partial(upward_kernel, part is not None),
        out_shape=shapes,
        in_specs=[VM] * len(args),
        out_specs=[VM] * len(shapes),
        scratch_shapes=scratch,
        cost_estimate=cost(15),
        compiler_params=pltpu.CompilerParams(
            collective_id=cid, has_side_effects=True, vmem_limit_bytes=LIMIT
        ),
    )(*args)


def rows_kernel(
    rows_ref, base_ref, wq, wk, wv, out_ref, vq, vk, vv, got, mine, ts, tr, gs, gr, own
):
    fetches = [
        pltpu.make_async_copy(src, dst, own.at[i])
        for i, (src, dst) in enumerate(((wq, vq), (wk, vk), (wv, vv)))
    ]
    for fetch in fetches:
        fetch.start()
    me = lax.axis_index("tp")
    peers = others("tp")
    greet([{"tp": peer} for peer in peers])
    for copy in swap_start(rows_ref, got, "tp", ts, tr):
        copy.wait()
    total = rows_ref[me].astype(f32)
    for peer in peers:
        total = total + got[peer].astype(f32)
    quarter = rows_ref.shape[2]
    base = base_ref[:, pl.ds(pl.multiple_of(me * quarter, 128), quarter)]
    mine[...] = (base.astype(f32) + total).astype(bf16)
    copies = [
        remote(mine, out_ref.at[me], gs.at[d], gr.at[d], {"tp": peer})
        for d, peer in enumerate(peers)
    ]
    for copy in copies:
        copy.start()
    out_ref[me] = mine[...]
    for copy in copies + fetches:
        copy.wait()


def final_kernel(
    part_ref, stream_ref, place_ref, out_ref, got, send, mine, ts, tr, ss, sr, cs, cr, ps, pr
):
    me = lax.axis_index("tp")
    seq = lax.axis_index("seq")
    peers = others("tp")
    groups = lax.axis_size("tp") // 2
    high, low = me // 2, lax.rem(me, 2)
    ranks, cap, size = send.shape
    greet([{"tp": peer} for peer in peers] + [{"seq": peer} for peer in others("seq")])
    for copy in swap_start(part_ref, got, "tp", ts, tr):
        copy.wait()
    total = stream_ref[me].astype(f32) + part_ref[me].astype(f32)
    for peer in peers:
        total = total + got[peer].astype(f32)
    main = total.astype(bf16)
    send[...] = t_mm(place_ref[...], main).astype(bf16).reshape(ranks, cap, size)
    copies = swap_start(send, mine, "seq", ss, sr)
    mine[seq] = send[seq]

    def spot(e, d):
        column = (lax.rem(high - e + groups, groups) * 2 + low) * size
        return out_ref.at[lax.rem(seq - d + ranks, ranks), :, pl.ds(pl.multiple_of(column, 128), size)]

    def held(e, d):
        return mine.at[lax.rem(seq - d + ranks, ranks)] if e == 0 else spot(e, d)

    def direct(e, d):
        device = {"tp": lax.rem(high + e, groups) * 2 + low}
        return remote(held(0, d), spot(0, d), cs.at[e, d], cr.at[e, d], device)

    def pair(e, d):
        device = {"tp": high * 2 + 1 - low}
        return remote(held(e, d), spot(e, d), ps.at[e, d], pr.at[e, d], device)

    for d in range(ranks):
        if d > 0:
            copies[d - 1].wait_recv()
        for e in range(1, groups):
            direct(e, d).start()
        pair(0, d).start()
    for d in range(ranks):
        for e in range(1, groups):
            direct(e, d).wait_recv()
            pair(e, d).start()
    out_ref[:, :, pl.ds(pl.multiple_of(me * size, 128), size)] = mine[...]
    for d in range(ranks):
        if d > 0:
            copies[d - 1].wait_send()
        for e in range(groups):
            if e > 0:
                direct(e, d).wait_send()
            pair(e, d).wait()


def on_device(
    byte_states, flags, stretch_owner, log_decay, w_x, w_z, w_bc, w_out, pad_vector, w_q, w_k, w_v, w_o
):
    rows, width = byte_states.shape
    heads = log_decay.shape[1]
    inner = w_x.shape[1]
    state_n = w_bc.shape[1] // 2
    ranks = lax.axis_size("seq")
    split = lax.axis_size("tp")
    count = stretch_owner.shape[0]
    quarter = width // split
    cap = max(2, 2 * count // ranks)
    wide = w_q.shape[0]
    shape = jax.ShapeDtypeStruct

    def call(kernel, outs, *args, far=(), scratch=(), us=2, grant=3 * LIMIT):
        specs = [HBM if i in far else VM for i in range(len(args))]
        return pl.pallas_call(
            kernel,
            out_shape=outs,
            in_specs=specs,
            out_specs=[VM] * len(outs),
            scratch_shapes=list(scratch),
            cost_estimate=cost(us),
            compiler_params=pltpu.CompilerParams(vmem_limit_bytes=grant),
        )(*args)

    mixed, gate, cmat, grow, state = call(
        local_kernel,
        [
            shape((rows, inner), f32),
            shape((rows, inner), f32),
            shape((rows, state_n), bf16),
            shape((rows, heads), f32),
            shape((heads * state_n + 48, inner // heads), bf16),
        ],
        byte_states, w_x, w_z, w_bc, log_decay.T,
        far=(0, 1, 2, 3),
        scratch=[pltpu.VMEM(a.shape, bf16) for a in (byte_states, w_x, w_z, w_bc)] + [DMA((4, 2))],
        us=4,
        grant=64000000,
    )
    (every,) = upward(state, cid=1)
    part, partial_rows, base = call(
        functools.partial(encode_kernel, split),
        [
            shape((split, rows, quarter), bf16),
            shape((split, count, quarter), bf16),
            shape((count, width), bf16),
        ],
        every, mixed, gate, cmat, grow, w_out, flags.reshape(1, rows), byte_states,
    )
    peers = max(split - 1, 1)
    stretch_rows, w_q, w_k, w_v = pl.pallas_call(
        rows_kernel,
        out_shape=[shape((split, count, quarter), bf16)]
        + [shape(w.shape, w.dtype) for w in (w_q, w_k, w_v)],
        in_specs=[VM] * 2 + [HBM] * 3,
        out_specs=[VM] * 4,
        scratch_shapes=[
            pltpu.VMEM((split, count, quarter), bf16),
            pltpu.VMEM((count, quarter), bf16),
        ]
        + [DMA((peers,))] * 4
        + [DMA((3,))],
        cost_estimate=cost(10),
        compiler_params=pltpu.CompilerParams(
            collective_id=2, has_side_effects=True, vmem_limit_bytes=LIMIT
        ),
    )(partial_rows, base, w_q, w_k, w_v)
    queries, kv, stream, place = call(
        project_kernel,
        [
            shape((count, w_q.shape[1]), bf16),
            shape((count, 2 * w_k.shape[1]), bf16),
            shape((split, count, wide // split), bf16),
            shape((count, ranks * cap), bf16),
        ],
        stretch_rows, pad_vector.reshape(1, -1), w_q, w_k, w_v, stretch_owner,
    )
    every_kv, got = upward(kv, part, cid=3)
    group = math.gcd(ranks, 8)
    partial_main, enc_out = call(
        functools.partial(attend_kernel, group, split),
        [shape((split, count, wide // split), bf16), shape((rows, quarter), bf16)],
        queries, every_kv, w_o, part, got, byte_states,
        far=(5,),
        scratch=[pltpu.VMEM((rows, quarter), bf16), DMA],
    )
    main_out = pl.pallas_call(
        final_kernel,
        out_shape=shape((ranks, cap, wide), bf16),
        in_specs=[VM] * 3,
        out_specs=VM,
        scratch_shapes=[
            pltpu.VMEM((split, count, wide // split), bf16),
            pltpu.VMEM((ranks, cap, wide // split), bf16),
            pltpu.VMEM((ranks, cap, wide // split), bf16),
        ]
        + [DMA((peers,))] * 2
        + [DMA((max(ranks - 1, 1),))] * 2
        + [DMA((split // 2, ranks))] * 4,
        cost_estimate=cost(20),
        compiler_params=pltpu.CompilerParams(
            collective_id=4, has_side_effects=True, vmem_limit_bytes=LIMIT
        ),
    )(partial_main, stream, place)
    main_out = main_out.reshape(ranks * cap, wide)
    return (enc_out, main_out)


def solution(mesh):
    placed = (
        P("seq", None),
        P("seq"),
        P("seq", None),
        P("seq", "tp"),
        P(None, "tp"),
        P(None, "tp"),
        P(),
        P("tp", None),
        P(),
        P(None, "tp"),
        P(None, "tp"),
        P(None, "tp"),
        P("tp", None),
    )
    return jax.shard_map(
        on_device,
        mesh=mesh,
        in_specs=placed,
        out_specs=(P("seq", "tp"), P("seq", None)),
        check_vma=False,
    )
```

```python
import functools
import math

import jax
import jax.numpy as jnp
from jax import lax
from jax.experimental import pallas as pl
from jax.experimental.pallas import tpu as pltpu
from jax.sharding import PartitionSpec as P

HD = 128
eps = 1e-05
f32 = jnp.float32
bf16 = jnp.bfloat16
MESH = pl.DeviceIdType.MESH
VM = pl.BlockSpec(memory_space=pltpu.VMEM)
HBM = pl.BlockSpec(memory_space=pltpu.HBM)
DMA = pltpu.SemaphoreType.DMA
LIMIT = 8 * 1024 * 1024


def cost(us):
    return pl.CostEstimate(flops=us * 10**9, bytes_accessed=us * 3 * 10**6, transcendentals=0)


def mm(a, b):
    return jnp.dot(a, b, preferred_element_type=f32)


def mm_t(a, b):
    return lax.dot_general(a, b, (((1,), (1,)), ((), ())), preferred_element_type=f32)


def t_mm(a, b):
    return lax.dot_general(a, b, (((0,), (0,)), ((), ())), preferred_element_type=f32)


def three(a):
    hi = a.astype(bf16)
    rest = a - hi.astype(f32)
    mid = rest.astype(bf16)
    low = (rest - mid.astype(f32)).astype(bf16)
    return hi, mid, low


def iota(shape, dim):
    return lax.broadcasted_iota(jnp.int32, shape, dim)


def local_kernel(
    bytes_hbm, wx_hbm, wz_hbm, wbc_hbm, decay_ref, mixed_ref, gate_ref, c_ref, grow_ref, state_ref,
    bytes_ref, wx_ref, wz_ref, wbc_ref, sems,
):
    fetches = []
    for i, (src, dst) in enumerate(
        ((bytes_hbm, bytes_ref), (wbc_hbm, wbc_ref), (wx_hbm, wx_ref), (wz_hbm, wz_ref))
    ):
        half = src.shape[0] // 2
        for j in range(2):
            span = pl.ds(j * half, half)
            copy = pltpu.make_async_copy(src.at[span], dst.at[span], sems.at[i, j])
            copy.start()
            fetches.append(copy)

    def ready(i):
        fetches[2 * i].wait()
        fetches[2 * i + 1].wait()

    rows = bytes_ref.shape[0]
    heads = decay_ref.shape[0]
    state_n = wbc_ref.shape[1] // 2
    p = wx_ref.shape[1] // heads
    parts = three(decay_ref[...])
    lower = (iota((rows, rows), 0) >= iota((rows, rows), 1)).astype(f32).astype(bf16)
    upper = (iota((rows, rows), 0) <= iota((rows, rows), 1)).astype(f32).astype(bf16)
    ones = jnp.ones((rows, state_n), bf16)
    cum = sum(mm_t(lower, part) for part in parts)
    cum_row = sum(mm(part, upper) for part in parts)
    total = sum(mm(part, ones) for part in parts)
    ready(0)
    wide = bytes_ref[...].astype(f32)
    normed = (wide * lax.rsqrt(jnp.mean(wide * wide, axis=-1, keepdims=True) + eps)).astype(bf16)
    ready(1)
    bc = mm(normed, wbc_ref[...]).astype(bf16)
    bmat, cmat = bc[:, :state_n], bc[:, state_n:]
    c_ref[...] = cmat
    ready(2)
    xs = mm(normed, wx_ref[...]).astype(bf16)
    last = cum[rows - 1 : rows, :]
    grow_ref[...] = jnp.exp(cum)
    tail = jnp.exp(last - cum)
    for h in range(heads):
        scaled = (xs[:, h * p : (h + 1) * p].astype(f32) * tail[:, h : h + 1]).astype(bf16)
        state_ref[h * state_n : (h + 1) * state_n, :] = t_mm(bmat, scaled).astype(bf16)
    pieces = [piece.astype(f32) for piece in three(total)]
    filler = jnp.zeros((16 - heads % 16, state_n), f32)
    for i, piece in enumerate(pieces):
        start = heads * state_n + 16 * i
        state_ref[start : start + 16, :] = jnp.concatenate([piece, filler], axis=0).astype(bf16)
    ready(3)
    z = mm(normed, wz_ref[...])
    gate_ref[...] = z * jax.nn.sigmoid(z)
    half = rows // 2
    for r in range(2):
        lo, hi = r * half, (r + 1) * half
        inter = mm_t(cmat[lo:hi], bmat[:hi])
        causal = iota((half, hi), 0) + lo >= iota((half, hi), 1)
        for h in range(heads):
            spans = cum[lo:hi, h : h + 1] - cum_row[h : h + 1, :hi]
            mixing = (inter * jnp.exp(jnp.where(causal, spans, -1e30))).astype(bf16)
            mixed_ref[lo:hi, h * p : (h + 1) * p] = mm(mixing, xs[:hi, h * p : (h + 1) * p])


def encode_kernel(
    split, every_ref, mixed_ref, gate_ref, c_ref, grow_ref, wout_ref, flags_ref, bytes_ref,
    part_ref, rows_ref, base_ref,
):
    me = lax.axis_index("seq")
    rows, heads = grow_ref.shape
    state_n = c_ref.shape[1]
    p = mixed_ref.shape[1] // heads
    cmat = c_ref[...]
    scaled = []

    def step(k, state):
        block = every_ref[k].astype(f32)
        size = heads * state_n
        total = block[size : size + 16] + block[size + 16 : size + 32] + block[size + 32 :]
        shrink = jnp.exp(total)
        return tuple(
            state[h] * shrink[h : h + 1] + block[h * state_n : (h + 1) * state_n]
            for h in range(heads)
        )

    state = lax.fori_loop(
        0, me, step, tuple(jnp.zeros((state_n, p), f32) for _ in range(heads))
    )
    for h in range(heads):
        cols = slice(h * p, (h + 1) * p)
        mixed = mixed_ref[:, cols] + mm(cmat, state[h].astype(bf16)) * grow_ref[:, h : h + 1]
        gated = mixed * gate_ref[:, cols]
        norm = lax.rsqrt(jnp.mean(gated * gated, axis=1, keepdims=True) + eps)
        scaled.append((gated * norm).astype(bf16))
    scaled = jnp.concatenate(scaled, axis=1)
    count = rows_ref.shape[1]
    flags = flags_ref[...]
    upper = (iota((rows, rows), 0) <= iota((rows, rows), 1)).astype(f32).astype(bf16)
    many = jnp.broadcast_to(flags.astype(f32), (16, rows)).astype(bf16)
    rank = mm(many, upper)[0:1, :].astype(jnp.int32) - 1
    hit = (rank == iota((count, rows), 0)) & (flags == 1)
    picker = jnp.where(hit, 1.0, 0.0).astype(bf16)
    base_ref[...] = mm(picker, bytes_ref[...]).astype(bf16)
    quarter = wout_ref.shape[1] // split
    for q in range(split):
        part = mm(scaled, wout_ref[:, q * quarter : (q + 1) * quarter]).astype(bf16)
        part_ref[q] = part
        rows_ref[q] = mm(picker, part).astype(bf16)


def project_kernel(rows_ref, pad_ref, wq_ref, wk_ref, wv_ref, owner_ref, q_ref, kv_ref, stream_ref, place_ref):
    split, count, quarter = rows_ref.shape
    pad = jnp.broadcast_to(pad_ref[...].astype(f32).reshape(1, -1), (count, pad_ref.shape[0])).astype(bf16)
    stream = jnp.concatenate([rows_ref[q] for q in range(split)] + [pad], axis=1)
    size = stream.shape[1] // split
    for q in range(split):
        stream_ref[q] = stream[:, q * size : (q + 1) * size]
    wide = stream.astype(f32)
    norm = (wide * lax.rsqrt(jnp.mean(wide * wide, axis=-1, keepdims=True) + eps)).astype(bf16)
    q_ref[...] = mm(norm, wq_ref[...]).astype(bf16)
    width = wk_ref.shape[1]
    kv_ref[:, :width] = mm(norm, wk_ref[...]).astype(bf16)
    kv_ref[:, width:] = mm(norm, wv_ref[...]).astype(bf16)
    slots = place_ref.shape[0]
    owner = owner_ref[...]
    ranks = -(-lax.axis_size("seq") // 128) * 128
    hot = jnp.where(owner == iota((ranks, count), 0), 1.0, 0.0)
    strict = jnp.where(iota((count, count), 0) < iota((count, count), 1), 1.0, 0.0)
    before = mm(hot.astype(bf16), strict.astype(bf16))
    order = jnp.sum(before * hot, axis=0, keepdims=True).astype(jnp.int32)
    cap = slots // lax.axis_size("seq")
    slot = owner * cap + order
    place_ref[...] = jnp.where(slot == iota((slots, count), 0), 1.0, 0.0).astype(bf16)


def attend_kernel(
    group, split, q_ref, all_ref, wo_ref, part_ref, got_ref, bytes_hbm, out_ref, enc_ref, base, sem
):
    me = lax.axis_index("seq")
    col = lax.axis_index("tp")
    quarter = base.shape[1]
    span = pl.ds(pl.multiple_of(col * quarter, 128), quarter)
    fetch = pltpu.make_async_copy(bytes_hbm.at[:, span], base, sem)
    fetch.start()
    ranks, count, width2 = all_ref.shape
    width = width2 // 2
    heads = width // HD
    scale = 1.0 / math.sqrt(HD)
    keys = group * count

    def chunk(c, carry):
        start = c * group
        blocks = all_ref[pl.ds(start, group)]
        blocks = blocks.reshape(keys, width2)
        key_pos = start * count + iota((count, keys), 1)
        allowed = key_pos <= me * count + iota((count, keys), 0)
        seen = start * count + iota((keys, width), 0) < (me + 1) * count
        values = jnp.where(seen, blocks[:, width:], jnp.zeros((), bf16))
        new = []
        for h in range(heads):
            best, total, accum = carry[h]
            cols = slice(h * HD, (h + 1) * HD)
            scores = mm_t(q_ref[:, cols], blocks[:, cols]) * scale
            scores = jnp.where(allowed, scores, -1e30)
            top = jnp.maximum(best, jnp.max(scores, axis=1, keepdims=True))
            shrink = jnp.exp(best - top)
            expo = jnp.exp(scores - top)
            total = total * shrink + jnp.sum(expo, axis=1, keepdims=True)
            accum = accum * shrink + mm(expo.astype(bf16), values[:, cols])
            new.append((top, total, accum))
        return tuple(new)

    start = tuple(
        (jnp.full((count, 1), -1e30, f32), jnp.zeros((count, 1), f32), jnp.zeros((count, HD), f32))
        for _ in range(heads)
    )
    if ranks == group:
        done = chunk(0, start)
    else:
        done = lax.fori_loop(0, me // group + 1, chunk, start)
    attended = jnp.concatenate([(a / t).astype(bf16) for _, t, a in done], axis=1)
    size = wo_ref.shape[1] // split
    for q in range(split):
        out_ref[q] = mm(attended, wo_ref[:, q * size : (q + 1) * size]).astype(bf16)
    fetch.wait()
    summed = part_ref[col].astype(f32)
    for d in range(1, split):
        summed = summed + got_ref[lax.rem(col + d, split)].astype(f32)
    enc_ref[...] = (base[...].astype(f32) + summed).astype(bf16)


def greet(devices):
    barrier = pltpu.get_barrier_semaphore()
    for device in devices:
        pl.semaphore_signal(barrier, inc=1, device_id=device, device_id_type=MESH)
    pl.semaphore_wait(barrier, len(devices))


def others(axis):
    me, n = lax.axis_index(axis), lax.axis_size(axis)
    return [lax.rem(me + d, n) for d in range(1, n)]


def remote(src, dst, send, recv, device):
    return pltpu.make_async_remote_copy(
        src_ref=src, dst_ref=dst, send_sem=send, recv_sem=recv, device_id=device, device_id_type=MESH
    )


def swap_start(src_ref, dst_ref, axis, send, recv):
    me = lax.axis_index(axis)
    copies = []
    for d, peer in enumerate(others(axis)):
        copy = remote(src_ref.at[peer], dst_ref.at[me], send.at[d], recv.at[d], {axis: peer})
        copy.start()
        copies.append(copy)
    return copies


def upward_kernel(with_swap, *refs):
    if with_swap:
        x_ref, part_ref, out_ref, got_ref, zs, zr, ws, wr, own, ts, tr = refs
    else:
        x_ref, out_ref, zs, zr, ws, wr, own = refs
    me = lax.axis_index("seq")
    n = lax.axis_size("seq")
    high, low = me // 2, lax.rem(me, 2)
    line = n // 2
    pieces = zs.shape[1]
    size = x_ref.shape[0] // pieces
    partner = {"seq": high * 2 + 1 - low}
    steps = sorted({1, line - 1} - {0}) if line > 1 else []
    devices = [{"seq": lax.rem(high + d, line) * 2 + low} for d in steps] + [partner]
    if with_swap:
        devices = devices + [{"tp": peer} for peer in others("tp")]
    greet(devices)
    mine = pltpu.make_async_copy(x_ref, out_ref.at[me], own)
    mine.start()

    def source(d, c):
        rows = pl.ds(c * size, size)
        return x_ref.at[rows] if d == 0 else out_ref.at[(high - d) * 2 + low, rows]

    def slot(d, c):
        return out_ref.at[(high - d) * 2 + low, pl.ds(c * size, size)]

    def up(d, c):
        device = {"seq": (high + 1) * 2 + low}
        return remote(source(d, c), slot(d, c), zs.at[d, c], zr.at[d + 1, c], device)

    def arrived(d, c):
        return remote(slot(d, c), slot(d, c), zs.at[d, c], zr.at[d, c], partner)

    def across(d, c):
        return remote(source(d, c), slot(d, c), ws.at[d, c], wr.at[d, c], partner)

    def send_on(d, c):
        if d < line - 1:

            @pl.when(high + 1 < line)
            def _():
                up(d, c).start()

        across(d, c).start()

    for c in range(pieces):
        send_on(0, c)
    if with_swap:
        swaps = swap_start(part_ref, got_ref, "tp", ts, tr)
    for d in range(1, line):

        @pl.when(high >= d)
        def _():
            for c in range(pieces):
                arrived(d, c).wait_recv()
                send_on(d, c)

    for d in range(line):

        @pl.when(high >= d)
        def _():
            for c in range(pieces):
                across(d, c).wait()
                if d < line - 1:

                    @pl.when(high + 1 < line)
                    def _():
                        up(d, c).wait_send()

    mine.wait()
    if with_swap:
        for copy in swaps:
            copy.wait()


def upward(x, part=None, cid=0):
    n = lax.axis_size("seq")
    line = max(n // 2, 1)
    fits = [c for c in (4, 5, 2, 1) if x.shape[0] % (16 * c) == 0 and c * line <= 32]
    pieces = fits[0]
    scratch = [DMA((line + 1, pieces))] * 4 + [DMA]
    shapes = [jax.ShapeDtypeStruct((n,) + x.shape, x.dtype)]
    args = [x]
    if part is not None:
        scratch += [DMA((part.shape[0],)), DMA((part.shape[0],))]
        shapes.append(jax.ShapeDtypeStruct(part.shape, part.dtype))
        args.append(part)
    return pl.pallas_call(
        functools.partial(upward_kernel, part is not None),
        out_shape=shapes,
        in_specs=[VM] * len(args),
        out_specs=[VM] * len(shapes),
        scratch_shapes=scratch,
        cost_estimate=cost(15),
        compiler_params=pltpu.CompilerParams(
            collective_id=cid, has_side_effects=True, vmem_limit_bytes=LIMIT
        ),
    )(*args)


def rows_kernel(
    rows_ref, base_ref, wq, wk, wv, out_ref, vq, vk, vv, got, mine, ts, tr, gs, gr, own
):
    fetches = [
        pltpu.make_async_copy(src, dst, own.at[i])
        for i, (src, dst) in enumerate(((wq, vq), (wk, vk), (wv, vv)))
    ]
    for fetch in fetches:
        fetch.start()
    me = lax.axis_index("tp")
    peers = others("tp")
    greet([{"tp": peer} for peer in peers])
    for copy in swap_start(rows_ref, got, "tp", ts, tr):
        copy.wait()
    total = rows_ref[me].astype(f32)
    for peer in peers:
        total = total + got[peer].astype(f32)
    quarter = rows_ref.shape[2]
    base = base_ref[:, pl.ds(pl.multiple_of(me * quarter, 128), quarter)]
    mine[...] = (base.astype(f32) + total).astype(bf16)
    copies = [
        remote(mine, out_ref.at[me], gs.at[d], gr.at[d], {"tp": peer})
        for d, peer in enumerate(peers)
    ]
    for copy in copies:
        copy.start()
    out_ref[me] = mine[...]
    for copy in copies + fetches:
        copy.wait()


def final_kernel(
    part_ref, stream_ref, place_ref, out_ref, got, send, mine, ts, tr, ss, sr, cs, cr, ps, pr
):
    me = lax.axis_index("tp")
    seq = lax.axis_index("seq")
    peers = others("tp")
    groups = lax.axis_size("tp") // 2
    high, low = me // 2, lax.rem(me, 2)
    ranks, cap, size = send.shape
    greet([{"tp": peer} for peer in peers] + [{"seq": peer} for peer in others("seq")])
    for copy in swap_start(part_ref, got, "tp", ts, tr):
        copy.wait()
    total = stream_ref[me].astype(f32) + part_ref[me].astype(f32)
    for peer in peers:
        total = total + got[peer].astype(f32)
    main = total.astype(bf16)
    send[...] = mm(place_ref[...], main).astype(bf16).reshape(ranks, cap, size)
    copies = swap_start(send, mine, "seq", ss, sr)
    mine[seq] = send[seq]

    def spot(e, d):
        column = (lax.rem(high - e + groups, groups) * 2 + low) * size
        return out_ref.at[lax.rem(seq - d + ranks, ranks), :, pl.ds(pl.multiple_of(column, 128), size)]

    def held(e, d):
        return mine.at[lax.rem(seq - d + ranks, ranks)] if e == 0 else spot(e, d)

    def direct(e, d):
        device = {"tp": lax.rem(high + e, groups) * 2 + low}
        return remote(held(0, d), spot(0, d), cs.at[e, d], cr.at[e, d], device)

    def pair(e, d):
        device = {"tp": high * 2 + 1 - low}
        return remote(held(e, d), spot(e, d), ps.at[e, d], pr.at[e, d], device)

    for d in range(ranks):
        if d > 0:
            copies[d - 1].wait_recv()
        for e in range(1, groups):
            direct(e, d).start()
        pair(0, d).start()
    for d in range(ranks):
        for e in range(1, groups):
            direct(e, d).wait_recv()
            pair(e, d).start()
    out_ref[:, :, pl.ds(pl.multiple_of(me * size, 128), size)] = mine[...]
    for d in range(ranks):
        if d > 0:
            copies[d - 1].wait_send()
        for e in range(groups):
            if e > 0:
                direct(e, d).wait_send()
            pair(e, d).wait()


def on_device(
    byte_states, flags, stretch_owner, log_decay, w_x, w_z, w_bc, w_out, pad_vector, w_q, w_k, w_v, w_o
):
    rows, width = byte_states.shape
    heads = log_decay.shape[1]
    inner = w_x.shape[1]
    state_n = w_bc.shape[1] // 2
    ranks = lax.axis_size("seq")
    split = lax.axis_size("tp")
    count = stretch_owner.shape[0]
    quarter = width // split
    cap = max(2, 2 * count // ranks)
    wide = w_q.shape[0]
    shape = jax.ShapeDtypeStruct

    def call(kernel, outs, *args, far=(), scratch=(), us=2, grant=3 * LIMIT):
        specs = [HBM if i in far else VM for i in range(len(args))]
        return pl.pallas_call(
            kernel,
            out_shape=outs,
            in_specs=specs,
            out_specs=[VM] * len(outs),
            scratch_shapes=list(scratch),
            cost_estimate=cost(us),
            compiler_params=pltpu.CompilerParams(vmem_limit_bytes=grant),
        )(*args)

    mixed, gate, cmat, grow, state = call(
        local_kernel,
        [
            shape((rows, inner), f32),
            shape((rows, inner), f32),
            shape((rows, state_n), bf16),
            shape((rows, heads), f32),
            shape((heads * state_n + 48, inner // heads), bf16),
        ],
        byte_states, w_x, w_z, w_bc, log_decay.T,
        far=(0, 1, 2, 3),
        scratch=[pltpu.VMEM(a.shape, bf16) for a in (byte_states, w_x, w_z, w_bc)] + [DMA((4, 2))],
        us=4,
        grant=64000000,
    )
    (every,) = upward(state, cid=1)
    part, partial_rows, base = call(
        functools.partial(encode_kernel, split),
        [
            shape((split, rows, quarter), bf16),
            shape((split, count, quarter), bf16),
            shape((count, width), bf16),
        ],
        every, mixed, gate, cmat, grow, w_out, flags.reshape(1, rows), byte_states,
    )
    peers = max(split - 1, 1)
    stretch_rows, w_q, w_k, w_v = pl.pallas_call(
        rows_kernel,
        out_shape=[shape((split, count, quarter), bf16)]
        + [shape(w.shape, w.dtype) for w in (w_q, w_k, w_v)],
        in_specs=[VM] * 2 + [HBM] * 3,
        out_specs=[VM] * 4,
        scratch_shapes=[
            pltpu.VMEM((split, count, quarter), bf16),
            pltpu.VMEM((count, quarter), bf16),
        ]
        + [DMA((peers,))] * 4
        + [DMA((3,))],
        cost_estimate=cost(10),
        compiler_params=pltpu.CompilerParams(
            collective_id=2, has_side_effects=True, vmem_limit_bytes=LIMIT
        ),
    )(partial_rows, base, w_q, w_k, w_v)
    queries, kv, stream, place = call(
        project_kernel,
        [
            shape((count, w_q.shape[1]), bf16),
            shape((count, 2 * w_k.shape[1]), bf16),
            shape((split, count, wide // split), bf16),
            shape((ranks * cap, count), bf16),
        ],
        stretch_rows, pad_vector, w_q, w_k, w_v, stretch_owner.reshape(1, count),
    )
    every_kv, got = upward(kv, part, cid=3)
    group = math.gcd(ranks, 8)
    partial_main, enc_out = call(
        functools.partial(attend_kernel, group, split),
        [shape((split, count, wide // split), bf16), shape((rows, quarter), bf16)],
        queries, every_kv, w_o, part, got, byte_states,
        far=(5,),
        scratch=[pltpu.VMEM((rows, quarter), bf16), DMA],
    )
    main_out = pl.pallas_call(
        final_kernel,
        out_shape=shape((ranks, cap, wide), bf16),
        in_specs=[VM] * 3,
        out_specs=VM,
        scratch_shapes=[
            pltpu.VMEM((split, count, wide // split), bf16),
            pltpu.VMEM((ranks, cap, wide // split), bf16),
            pltpu.VMEM((ranks, cap, wide // split), bf16),
        ]
        + [DMA((peers,))] * 2
        + [DMA((max(ranks - 1, 1),))] * 2
        + [DMA((split // 2, ranks))] * 4,
        cost_estimate=cost(20),
        compiler_params=pltpu.CompilerParams(
            collective_id=4, has_side_effects=True, vmem_limit_bytes=LIMIT
        ),
    )(partial_main, stream, place)
    main_out = main_out.reshape(ranks * cap, wide)
    return (enc_out, main_out)


def solution(mesh):
    placed = (
        P("seq", None),
        P("seq"),
        P("seq", None),
        P("seq", "tp"),
        P(None, "tp"),
        P(None, "tp"),
        P(),
        P("tp", None),
        P(),
        P(None, "tp"),
        P(None, "tp"),
        P(None, "tp"),
        P("tp", None),
    )
    return jax.shard_map(
        on_device,
        mesh=mesh,
        in_specs=placed,
        out_specs=(P("seq", "tp"), P("seq", None)),
        check_vma=False,
    )
```
